128 devices in a mesh: dp: 2 (over x_lo), phase: 16 (over z, y), tensor: 4 (over x_hi, core).
Axes of the slice: x: 4 (x_hi: 2, x_lo: 2; x = x_hi * 2 + x_lo), y: 4, z: 4, core: 2. Of those that a mesh axis runs over, the one named last changes fastest.
Arguments:
- tokens: bfloat16 [2, 2048, 8192], P('dp', 'phase', 'tensor'), may hold values from -6 to 6
- bc_proj: bfloat16 [2, 2048, 2, 2048], P('dp', 'phase', None, 'tensor'), may hold values from -0.3984375 to 0.3984375
- step_sizes: bfloat16 [2, 256, 1024], P('dp', 'phase', 'tensor'), may hold values from 0.5 to 2
- decay_rates: float32 [128], P('tensor'), may hold values from 6.1035156e-05 to 0.02
- direct_weight: float32 [128], P('tensor'), may hold values from 0.5 to 1.5
- norm_gain: float32 [8192], P('tensor'), may hold values from 0.1 to 1.9
- routes: int32 [2, 256, 1], P('dp', 'phase'), may hold values from 0 to 1; in each aligned block of 16 rows (0 to 15, 16 to 31, ..., all dimensions but the last counted through in order) at most 16 rows name the same one
- segments: int32 [2, 4096], P('dp', 'phase'), may hold values from 0 to 3, never falling along the last dimension, each value on 1 to 2048 neighbouring positions
Outputs:
- mixed: bfloat16 [2, 2048, 8192], P('dp', 'phase', 'tensor')
The draws below stay inside these ranges and needn't reach their ends.
Inputs may be any that keep to these rules, and one draw needn't show every extreme that they name: `routes`: no device sends more than 16 of its blocks to one data group. `segments`: document ids never fall along a row; each document covers 1 to 2048 positions, and one covers exactly 2048.
All inputs are finite; a program needn't handle non-finite values.
Results may differ from the reference program's by a relative error of at most 0.0075.
Values may be sent and summed in bfloat16 or wider, within the bound.
No kernel may reach another device: no remote copies, remote signals or barrier semaphores. Data moves between devices by JAX's collectives and lax.ppermute only.
A program may use at most 128 MiB of HBM per device.

```python
import math
import jax
import jax.numpy as jnp
import numpy as np
from jax import lax

HEAD_FEATURES = 64
STATE_ENTRIES = 256
LOCAL_HEADS = 128
SHARED_GROUPS = 8
BLOCK = 8
DOCUMENTS_PER_ROW = 4
BLK_DEV = 16
TOK_DEV = 128
CAP = 16
ROW_LENGTH = 4096
BLOCK_LENGTH = 128
N_DP = 2
N_PHASE = 16


def block_levels(key, shape, shards, low, largest):
    gain = 1.0
    for position, parts in shards:
        draws = jax.random.uniform(jax.random.fold_in(jax.random.fold_in(key, 6), position), (parts,), jnp.float32, low / len(shards), largest / len(shards))
        gain = gain * jnp.repeat(jnp.exp(draws), shape[position] // parts).reshape((-1,) + (1,) * (len(shape) - 1 - position))
    return gain


def split_up(count, total, most, slope):
    loads = [(1 << 20) // math.isqrt(grade ** slope) + 1 for grade in range(2, count + 1)]
    rest, given = total - most - (count - 1), [1] * (count - 1)
    while rest > 0:
        candidates = [i for i in range(count - 1) if given[i] < most]
        pool, budget = sum([loads[i] for i in candidates]), rest
        for i in candidates:
            extra = min(most - given[i], max(1, budget * loads[i] // pool), rest)
            given[i] = given[i] + extra
            rest = rest - extra
    return np.array([most] + given)


def ragged_sizes(key, number_of, total, reach, lean):
    if number_of == 2:
        one = jax.random.randint(key, (), max(1, total - reach), min(reach, total - 1) + 1)
        return jnp.stack([one, total - one])
    sizes = jnp.asarray(split_up(number_of, total, reach, lean), jnp.int32)
    couples = (number_of - 1) // 2
    donor, sink = sizes[1:1 + 2 * couples:2], sizes[2:2 + 2 * couples:2]
    room = jnp.minimum(donor - 1, reach - sink)
    shifted = jax.random.randint(jax.random.fold_in(key, 1), (couples,), 0, 1 << 20) % (room + 1)
    sizes = sizes.at[1:1 + 2 * couples:2].set(donor - shifted).at[2:2 + 2 * couples:2].set(sink + shifted)
    return sizes[jax.random.permutation(jax.random.fold_in(key, 2), number_of)]


def shared_out(own_key, own, number, rows, number_of, top, most, lean):
    sequence = jax.random.permutation(own_key, number_of)
    heavy_load, ordinary = shares(number_of, rows * top, most, lean, True), shares(number_of, rows * top, most, lean, False)
    places = jnp.arange(number_of)

    def named(sizes, offset_by):
        used = int((sizes > 0).sum())
        fixed = max(1, used // 4)
        shifted = fixed + (places - fixed + offset_by * (used - fixed)) % max(1, number_of - fixed)
        return jnp.zeros((number_of,), jnp.int32).at[sequence[jnp.where(places < fixed, places, shifted)]].set(jnp.asarray(sizes, jnp.int32))

    sizes = jnp.where(number % 4 == 0, named(heavy_load, number // 4), named(ordinary, number - number // 4 - 1))
    mixed = jax.random.permutation(jax.random.fold_in(own, 3), number_of)
    giver, taker = mixed[0:number_of // 2 * 2:2], mixed[1:number_of // 2 * 2:2]
    room = jnp.minimum(sizes[giver] - 1, most - sizes[taker]) // 2
    room = jnp.where((giver == sequence[0]) | (taker == sequence[0]) | (sizes[taker] == 0), 0, jnp.maximum(room, 0))
    shifted = jax.random.randint(jax.random.fold_in(own, 4), (number_of // 2,), 0, 1 << 20) % (room + 1)
    sizes = sizes.at[giver].add(-shifted).at[taker].add(shifted)
    labels = jnp.searchsorted(jnp.cumsum(sizes), jnp.arange(rows * top), side="right").astype(jnp.int32)
    table = labels.reshape(top, rows).T
    table = table[jax.random.permutation(jax.random.fold_in(own, 1), rows)]
    offset_by = jax.random.randint(jax.random.fold_in(own, 2), (rows, 1), 0, top)
    return jnp.take_along_axis(table, (jnp.arange(top)[None, :] + offset_by) % top, axis=1)


def shares(number_of, total, bound, slope, full):
    loads = [(1 << 20) // math.isqrt(rank ** slope) + 1 for rank in range(1, number_of + 1)]
    largest = bound if full else min(bound, max(-(-total // number_of), total * loads[0] // sum(loads)))
    least = 1 if total - largest >= number_of - 1 else 0
    given, spare = [largest] + [least] * (number_of - 1), total - largest - least * (number_of - 1)
    while spare > 0:
        free = [i for i in range(1, number_of) if given[i] < largest] or [i for i in range(1, number_of) if given[i] < bound]
        pool, budget = sum([loads[i] for i in free]), spare
        for i in free:
            addition = min(bound - given[i], max(1, budget * loads[i] // pool), spare)
            given[i] = given[i] + addition
            spare = spare - addition
    return np.array(given)


def gaussian(rng, dims, width, reach, cuts=(), held_as=jnp.bfloat16):
    loudness = block_levels(rng, dims, cuts, -0.22, 0.18) if cuts else 1.0
    drawn = jax.random.normal(rng, dims, jnp.float32) * width * loudness
    return jnp.minimum(jnp.maximum(drawn, -reach), reach).astype(held_as)


def setup_inputs(seed: int = 0) -> dict:
    splits = jax.random.split(jax.random.key(seed), 9)
    tokens = gaussian(splits[0], (N_DP, N_PHASE * TOK_DEV, LOCAL_HEADS * HEAD_FEATURES), 1.0, 6.0, ((0, 2), (1, 16), (2, 4)))
    bc_proj = gaussian(splits[1], (N_DP, N_PHASE * TOK_DEV, 2, SHARED_GROUPS * STATE_ENTRIES), 0.0625, 0.3984375, ((0, 2), (1, 16), (3, 4)))
    step_sizes = jnp.clip(jnp.exp(math.log(2.0) - 1.3862944 * jax.random.uniform(splits[2], (N_DP, N_PHASE * BLK_DEV, LOCAL_HEADS * BLOCK), jnp.float32) ** block_levels(splits[2], (N_DP, N_PHASE * BLK_DEV, LOCAL_HEADS * BLOCK), ((0, 2), (1, 16), (2, 4)), -0.2, 0.2)), 0.5, 2.0).astype(jnp.bfloat16)
    decay_rates = jnp.clip(jnp.exp(math.log(0.02) - 5.7920375 * jax.random.uniform(splits[3], (LOCAL_HEADS,), jnp.float32) ** block_levels(splits[3], (LOCAL_HEADS,), ((0, 4),), -0.2, 0.2)), 6.103515625e-05, 0.02)
    direct_weight = jnp.clip(0.5 + 1.0 * jax.random.uniform(splits[4], (LOCAL_HEADS,), jnp.float32) ** block_levels(splits[4], (LOCAL_HEADS,), ((0, 4),), -0.2, 0.2), 0.5, 1.5)
    norm_gain = jnp.clip(1.0 + 0.18 * jax.random.normal(splits[5], (LOCAL_HEADS * HEAD_FEATURES,), jnp.float32), 0.1, 1.9)
    routes_keys = jax.random.split(jax.random.fold_in(splits[6], 1), N_DP * (N_PHASE * BLK_DEV) // BLK_DEV)
    routes_turns = jax.random.permutation(jax.random.fold_in(splits[6], 3), N_DP * (N_PHASE * BLK_DEV) // BLK_DEV)
    routes = jax.vmap(lambda own, number: shared_out(jax.random.fold_in(splits[6], 2), own, number, BLK_DEV, N_DP, 1, CAP, 2))(routes_keys, routes_turns).reshape((N_DP, N_PHASE * BLK_DEV, 1))
    segments = jax.vmap(lambda own: jnp.searchsorted(jnp.cumsum(ragged_sizes(own, DOCUMENTS_PER_ROW, ROW_LENGTH, ROW_LENGTH // 2, 0)), jnp.arange(ROW_LENGTH), side="right"))(jax.random.split(splits[7], N_DP)).reshape((N_DP, ROW_LENGTH)).astype(jnp.int32)
    return dict(tokens=tokens, bc_proj=bc_proj, step_sizes=step_sizes, decay_rates=decay_rates, direct_weight=direct_weight, norm_gain=norm_gain, routes=routes, segments=segments)


EPSILON = 1e-05
PRECISE = lax.Precision.HIGHEST

def stretch_pass(carry_state, prior_id, x_stretch, b_stretch, c_stretch, dt_stretch, doc_ids, decay_rates):
    span_len = x_stretch.shape[0]
    head_count = x_stretch.shape[1]
    groups = b_stretch.shape[1]
    per_group = head_count // groups
    log_decay = jnp.cumsum(-decay_rates[:, None] * dt_stretch, axis=1)
    positions = jnp.arange(span_len)
    same_doc = (doc_ids[:, None] == doc_ids[None, :]) & (positions[:, None] >= positions[None, :])
    gaps = jnp.minimum(log_decay[:, :, None] - log_decay[:, None, :], 0.0)
    decay_mat = jnp.where(same_doc[None], jnp.exp(gaps), 0.0) * dt_stretch[:, None, :]
    scores = jnp.einsum('ign,jgn->gij', c_stretch, b_stretch, precision=PRECISE)
    weights = decay_mat.reshape(groups, per_group, span_len, span_len) * scores[:, None]
    x_groups = x_stretch.reshape(span_len, groups, per_group, -1)
    inside = jnp.einsum('gkij,jgkp->igkp', weights, x_groups, precision=PRECISE)
    state_groups = carry_state.reshape(groups, per_group, carry_state.shape[1], carry_state.shape[2])
    carried = jnp.einsum('ign,gkpn->igkp', c_stretch, state_groups, precision=PRECISE)
    keep_in = jnp.where(doc_ids[None, :] == prior_id, jnp.exp(log_decay), 0.0)
    result = inside + keep_in.T.reshape(span_len, groups, per_group)[..., None] * carried
    last_id = doc_ids[-1]
    tail_decay = jnp.where(doc_ids[None, :] == last_id, jnp.exp(log_decay[:, -1:] - log_decay), 0.0) * dt_stretch
    scaled = x_groups * tail_decay.T.reshape(span_len, groups, per_group)[..., None]
    update = jnp.einsum('jgkp,jgn->gkpn', scaled, b_stretch, precision=PRECISE).reshape(carry_state.shape)
    through = jnp.where(prior_id == last_id, jnp.exp(log_decay[:, -1]), 0.0)
    new_state = through[:, None, None] * carry_state + update
    return (new_state, last_id, result.reshape(span_len, head_count, -1))

def row_pass(input_row, b_row, c_row, dt_row, doc_row, decay_rates, direct_weight):
    block_count = ROW_LENGTH // BLOCK_LENGTH
    input_single = input_row.astype(jnp.float32).reshape(ROW_LENGTH, LOCAL_HEADS, HEAD_FEATURES)
    x_stretches = input_single.reshape(block_count, BLOCK_LENGTH, LOCAL_HEADS, HEAD_FEATURES)
    b_stretches = b_row.astype(jnp.float32).reshape(block_count, BLOCK_LENGTH, SHARED_GROUPS, STATE_ENTRIES)
    c_stretches = c_row.astype(jnp.float32).reshape(block_count, BLOCK_LENGTH, SHARED_GROUPS, STATE_ENTRIES)
    dt_stretches = dt_row.reshape(LOCAL_HEADS, block_count, BLOCK_LENGTH).transpose(1, 0, 2)
    doc_stretches = doc_row.reshape(block_count, BLOCK_LENGTH)

    def advance(carry, pieces):
        new_state, last_id, result = stretch_pass(carry[0], carry[1], pieces[0], pieces[1], pieces[2], pieces[3], pieces[4], decay_rates)
        return ((new_state, last_id), result)
    start_carry = (jnp.zeros((LOCAL_HEADS, HEAD_FEATURES, STATE_ENTRIES), jnp.float32), jnp.array(-1.0, jnp.float32))
    _, scan_results = lax.scan(advance, start_carry, (x_stretches, b_stretches, c_stretches, dt_stretches, doc_stretches))
    output_row = scan_results.reshape(ROW_LENGTH, LOCAL_HEADS, HEAD_FEATURES) + direct_weight[None, :, None] * input_single
    return output_row.astype(jnp.bfloat16).reshape(ROW_LENGTH, LOCAL_HEADS * HEAD_FEATURES)

def reference(tokens, bc_proj, step_sizes, decay_rates, direct_weight, norm_gain, routes, segments):
    feature_width = LOCAL_HEADS * HEAD_FEATURES
    targets = routes[:, :, 0].reshape(N_DP, N_PHASE, BLK_DEV).astype(jnp.int32)
    positions = jnp.arange(BLK_DEV)
    earlier = positions[:, None] > positions[None, :]
    slot_rank = lax.optimization_barrier(jnp.sum((targets[..., :, None] == targets[..., None, :]) & earlier, axis=-1)).astype(jnp.int32)
    source_ids = jnp.arange(N_DP).astype(jnp.int32)[:, None, None]
    phase_ids = jnp.arange(N_PHASE).astype(jnp.int32)[None, :, None]
    x_blocks = tokens.reshape(N_DP, N_PHASE, BLK_DEV, BLOCK, feature_width)
    input_rows = jnp.zeros((N_DP, N_PHASE, N_DP, CAP, BLOCK, feature_width), jnp.bfloat16).at[targets, phase_ids, source_ids, slot_rank].set(x_blocks)
    bc_blocks = bc_proj.reshape(N_DP, N_PHASE, BLK_DEV, BLOCK, 2, SHARED_GROUPS, STATE_ENTRIES)
    input_output_rows = jnp.zeros((N_DP, N_PHASE, N_DP, CAP, BLOCK, 2, SHARED_GROUPS, STATE_ENTRIES), jnp.bfloat16).at[targets, phase_ids, source_ids, slot_rank].set(bc_blocks)
    dt_blocks = step_sizes.reshape(N_DP, N_PHASE, BLK_DEV, LOCAL_HEADS, BLOCK)
    step_size_rows = jnp.zeros((N_DP, N_PHASE, N_DP, CAP, LOCAL_HEADS, BLOCK), jnp.bfloat16).at[targets, phase_ids, source_ids, slot_rank].set(dt_blocks)
    input_rows = input_rows.reshape(N_DP, ROW_LENGTH, feature_width)
    input_proj_rows = input_output_rows[:, :, :, :, :, 0].reshape(N_DP, ROW_LENGTH, SHARED_GROUPS, STATE_ENTRIES)
    output_proj_rows = input_output_rows[:, :, :, :, :, 1].reshape(N_DP, ROW_LENGTH, SHARED_GROUPS, STATE_ENTRIES)
    step_size_rows = step_size_rows.transpose(0, 4, 1, 2, 3, 5).reshape(N_DP, LOCAL_HEADS, ROW_LENGTH).astype(jnp.float32)
    doc_rows = segments.astype(jnp.float32)

    def one_row(pieces):
        return row_pass(pieces[0], pieces[1], pieces[2], pieces[3], pieces[4], decay_rates, direct_weight)
    y_rows = lax.map(one_row, (input_rows, input_proj_rows, output_proj_rows, step_size_rows, doc_rows))
    y_slots = y_rows.reshape(N_DP, N_PHASE, N_DP, CAP, BLOCK, feature_width)
    moved = y_slots[targets, phase_ids, source_ids, slot_rank]
    moved = moved.reshape(N_DP, N_PHASE * BLK_DEV * BLOCK, feature_width).astype(jnp.float32)
    square_sums = lax.optimization_barrier(jnp.sum(moved * moved, axis=-1, keepdims=True))
    mixed = moved * lax.rsqrt(square_sums / feature_width + EPSILON) * norm_gain
    return mixed.astype(jnp.bfloat16)
```

```python
import jax
import jax.numpy as jnp
from jax import lax
from jax.experimental import pallas as pl
from jax.experimental.pallas import tpu as pltpu
from jax.sharding import Mesh, PartitionSpec as P

EPSILON = 1e-05
F32 = jnp.float32
BF16 = jnp.bfloat16
HIGH = lax.Precision.HIGHEST
TOK = 128
PEERS = 8
SPAN = TOK * PEERS
WIDE = 256
AUX = 8


def dot(a, b, dims, precision=None):
    return lax.dot_general(a, b, (dims, ((), ())), precision=precision, preferred_element_type=F32)


def iota(shape, dim):
    return lax.broadcasted_iota(jnp.int32, shape, dim)


def ones_where(cond, dtype=F32):
    return jnp.where(cond, 1.0, 0.0).astype(dtype)


def pack_kernel(where_ref, tok_ref, b_ref, c_ref, dt_ref, route_ref, seg_ref, out_ref):
    block_of = ones_where(iota((16, TOK), 1) // 8 == iota((16, TOK), 0), BF16)
    spread = dot(dt_ref[...], block_of, ((0,), (0,)))
    same_u = iota((256, TOK), 0) % 8 == iota((256, TOK), 1) % 8
    spread = jnp.where(same_u, spread, 0.0).astype(BF16)
    head_of = ones_where(iota((32, 256), 1) // 8 == iota((32, 256), 0), BF16)
    dt_rows = dot(head_of, spread, ((1,), (0,)))
    route = jnp.broadcast_to(route_ref[...].astype(F32), (16, TOK)).astype(BF16)
    route_row = dot(route, block_of, ((0,), (0,)))
    route_col = dot(block_of, route, ((0,), (0,)))
    ahead = (route_row == route_col) & (iota((TOK, TOK), 0) < iota((TOK, TOK), 1))
    place = jnp.sum(ones_where(ahead), axis=0, keepdims=True) + (where_ref[0] * TOK).astype(F32)
    segs = seg_ref[...]
    lane = iota((1, TOK), 1)
    starts = jnp.zeros((1, TOK), F32)
    for k in range(3):
        starts = jnp.where(lane == k, jnp.sum(ones_where(segs < k + 1), axis=1, keepdims=True), starts)
    row = iota((AUX, TOK), 0)
    for o in range(PEERS):
        g = o // 4
        out_ref[o, :TOK, 0:WIDE] = tok_ref[:, o * WIDE : (o + 1) * WIDE]
        out_ref[o, :TOK, WIDE : 2 * WIDE] = b_ref[:, g * WIDE : (g + 1) * WIDE]
        out_ref[o, :TOK, 2 * WIDE : 3 * WIDE] = c_ref[:, g * WIDE : (g + 1) * WIDE]
        aux = jnp.where(row == 4, route_row[0:1], jnp.where(row == 5, place, starts))
        for h in range(4):
            aux = jnp.where(row == h, dt_rows[o * 4 + h : o * 4 + h + 1], aux)
        out_ref[o, TOK : TOK + AUX, :] = jnp.concatenate([aux.astype(BF16)] * 6, axis=1)


def rate_lanes(where_ref, ref):
    lane = iota((1, WIDE), 1) // 64
    first = where_ref[1] * 4
    out = jnp.full((1, WIDE), ref[first], F32)
    for h in range(1, 4):
        out = jnp.where(lane == h, ref[first + h], out)
    return out


def state_kernel(where_ref, rate_ref, r_ref, e_ref, f_ref, xs_ref, m_ref, fm_ref, meta_ref, dt_ref, bm_ref):
    rate = rate_lanes(where_ref, rate_ref)
    spread = ones_where(iota((AUX, WIDE), 1) // 64 == iota((AUX, WIDE), 0), BF16)
    pick_route = ones_where(iota((AUX, TOK), 0) == 4, BF16)
    pick_place = ones_where(iota((AUX, TOK), 0) == 5, BF16)
    starts = [[None] * 3, [None] * 3]
    rows, cols = [], []
    for q in range(PEERS):
        y, j = q // 2, q % 2
        aux = r_ref[j * 4 + y, TOK : TOK + AUX, 0:TOK]
        auxf = aux.astype(F32)
        dt_ref[q * TOK : (q + 1) * TOK, :] = dot(aux, spread, ((0,), (0,))).astype(BF16)
        rows.append((auxf[4:5], auxf[5:6] + y * 256.0))
        cols.append((dot(aux, pick_route, ((0,), (0,))), dot(aux, pick_place, ((0,), (0,))) + y * 256.0))
        for k in range(3):
            n = auxf[6:7, k : k + 1]
            starts[j][k] = n if starts[j][k] is None else starts[j][k] + n

    def key_of(route, place):
        second = route > 0.5
        doc = 4.0 * route
        for k in range(3):
            doc = doc + ones_where(place >= jnp.where(second, starts[1][k], starts[0][k]))
        return doc

    key_rows = [key_of(*p) for p in rows]
    key_cols = [key_of(*p) for p in cols]
    first, last = [], []
    for d in range(2):
        first.append(sum(ones_where(starts[d][k] <= 0.0) for k in range(3)))
        last.append(sum(ones_where(starts[d][k] <= SPAN - 1.0) for k in range(3)))
    causal = iota((TOK, TOK), 0) >= iota((TOK, TOK), 1)
    for i in range(PEERS):
        for jj in range(i + 1 + (i + 1) % 2):
            if jj > i:
                m = jnp.zeros((TOK, TOK), BF16)
            else:
                same = key_cols[i] == key_rows[jj]
                m = ones_where(same & causal if i == jj else same, BF16)
            m_ref[i * TOK : (i + 1) * TOK, jj * TOK : (jj + 1) * TOK] = m
        for d in range(2):
            fm_ref[i * TOK : (i + 1) * TOK, d * TOK : (d + 1) * TOK] = ones_where(
                key_cols[i] == first[d] + 4.0 * d, BF16
            )
            lm = ones_where(key_cols[i] == last[d] + 4.0 * d, BF16)
            src = (i % 2) * 4 + i // 2
            for half in range(2):
                bm_ref[d, i * TOK : (i + 1) * TOK, half * TOK : (half + 1) * TOK] = (
                    r_ref[src, :TOK, WIDE + half * TOK : WIDE + (half + 1) * TOK] * lm
                )
    for b in range(4):
        sl = slice(b * 256, (b + 1) * 256)
        total = dot(m_ref[sl, : (b + 1) * 256], dt_ref[: (b + 1) * 256, :], ((1,), (0,)))
        f_ref[sl, :] = jnp.exp(-rate * total)
        grow = jnp.exp(rate * total) * dt_ref[sl, :].astype(F32)
        for s in range(2):
            x = r_ref[s * 4 + b, :TOK, 0:WIDE].astype(F32)
            at = b * 256 + s * TOK
            xs_ref[at : at + TOK, :] = (x * grow[s * TOK : (s + 1) * TOK]).astype(BF16)
    row8 = iota((AUX, WIDE), 0)
    for d in range(2):
        total = jnp.zeros((AUX, WIDE), F32)
        for q in range(PEERS):
            lm = jnp.broadcast_to(ones_where(key_rows[q] == last[d] + 4.0 * d), (AUX, TOK)).astype(BF16)
            total = total + dot(lm, dt_ref[q * TOK : (q + 1) * TOK, :], ((1,), (0,)))
        through = jnp.exp(-rate * total)
        e = dot(bm_ref[d], xs_ref[...], ((0,), (0,))) * through[0:1]
        e_ref[d, 0:WIDE, :] = e.astype(BF16)
        e_ref[d, WIDE : WIDE + AUX, :] = jnp.where(row8 == 0, through, last[d]).astype(BF16)
    meta_ref[...] = jnp.where(iota((AUX, TOK), 0) == 0, first[0], first[1])


def inside_kernel(where_ref, weight_ref, r_ref, f_ref, xs_ref, m_ref, fm_ref, base_ref, cm_ref, b_ref, c_ref):
    weight = rate_lanes(where_ref, weight_ref)
    for q in range(PEERS):
        src = (q % 2) * 4 + q // 2
        sl = slice(q * TOK, (q + 1) * TOK)
        b_ref[sl, :] = r_ref[src, :TOK, WIDE : 2 * WIDE]
        c = r_ref[src, :TOK, 2 * WIDE : 3 * WIDE]
        c_ref[sl, :] = c
        for d in range(2):
            fm = fm_ref[sl, d * TOK : (d + 1) * TOK]
            for half in range(2):
                at = d * WIDE + half * TOK
                cm_ref[sl, at : at + TOK] = c[:, half * TOK : (half + 1) * TOK] * fm
    for i in range(4):
        si = slice(i * 256, (i + 1) * 256)
        acc = jnp.zeros((256, WIDE), F32)
        for j in range(i + 1):
            sj = slice(j * 256, (j + 1) * 256)
            s = dot(c_ref[si, :], b_ref[sj, :], ((1,), (1,)))
            w = (s * m_ref[si, sj].astype(F32)).astype(BF16)
            acc = acc + dot(w, xs_ref[sj, :], ((1,), (0,)))
        acc = acc * f_ref[si, :]
        for s in range(2):
            x = r_ref[s * 4 + i, :TOK, 0:WIDE].astype(F32)
            at = i * 256 + s * TOK
            base_ref[at : at + TOK, :] = acc[s * TOK : (s + 1) * TOK] + weight * x


def carry_kernel(base_ref, f_ref, cm_ref, e1_ref, e2_ref, meta_ref, y_ref, h_ref):
    for d in range(2):
        first = meta_ref[d : d + 1, 0:1]
        joined1 = e1_ref[d, WIDE + 1 : WIDE + 2, :].astype(F32) == first
        joined2 = joined1 & (e2_ref[d, WIDE + 1 : WIDE + 2, :].astype(F32) == first)
        through = jnp.where(joined2, e1_ref[d, WIDE : WIDE + 1, :].astype(F32), 0.0)
        near = jnp.where(joined1, e1_ref[d, 0:WIDE, :].astype(F32), 0.0)
        h_ref[d * WIDE : (d + 1) * WIDE, :] = (near + through * e2_ref[d, 0:WIDE, :].astype(F32)).astype(BF16)
    for q in range(PEERS):
        sl = slice(q * TOK, (q + 1) * TOK)
        y = base_ref[sl, :] + f_ref[sl, :] * dot(cm_ref[sl, :], h_ref[...], ((1,), (0,)))
        y_ref[(q % 2) * 4 + q // 2] = y.astype(BF16)


def square_kernel(y_ref, s_ref):
    acc = jnp.zeros((TOK, WIDE), F32)
    for o in range(PEERS):
        v = y_ref[o].astype(F32)
        acc = acc + v * v
    s_ref[...] = dot(jnp.ones((AUX, WIDE), F32), acc, ((1,), (1,)), HIGH)


def scale_kernel(y_ref, s0_ref, s1_ref, s2_ref, s3_ref, gain_ref, out_ref, *, features):
    total = (s0_ref[...] + s1_ref[...]) + (s2_ref[...] + s3_ref[...])
    pick = ones_where(iota((AUX, TOK), 0) == 0)
    col = dot(total, pick, ((0,), (0,)), HIGH)
    scale = lax.rsqrt(col / features + EPSILON)
    scale = jnp.concatenate([scale, scale], axis=1)
    for o in range(PEERS):
        sl = slice(o * WIDE, (o + 1) * WIDE)
        out_ref[:, sl] = (y_ref[o].astype(F32) * scale * gain_ref[:, sl]).astype(BF16)


VM = pl.BlockSpec(memory_space=pltpu.VMEM)
SM = pl.BlockSpec(memory_space=pltpu.SMEM)


def call(kernel, specs, outs, *args, scratch=()):
    out_shape = [jax.ShapeDtypeStruct(s, d) for s, d in outs]
    return pl.pallas_call(
        kernel,
        in_specs=specs,
        out_specs=[VM] * len(outs),
        out_shape=out_shape,
        scratch_shapes=list(scratch),
        name=kernel.__name__ if hasattr(kernel, "__name__") else "scale_kernel",
    )(*args)


def per_device(tokens, bc_proj, step_sizes, decay_rates, direct_weight, norm_gain, routes, segments):
    j = lax.axis_index("dp")
    y = lax.axis_index("y")
    where = jnp.stack([j, j * 4 + y]).astype(jnp.int32)
    b, c = bc_proj[0, :, 0], bc_proj[0, :, 1]
    (send,) = call(
        pack_kernel,
        [SM, VM, VM, VM, VM, VM, VM],
        [((PEERS, TOK + AUX, 3 * WIDE), BF16)],
        where, tokens[0], b, c, step_sizes[0], routes[0], segments,
    )
    got = lax.all_to_all(send, ("dp", "y"), split_axis=0, concat_axis=0, tiled=True)
    e, f, xs, m, fm, meta = call(
        state_kernel,
        [SM, SM, VM],
        [
            ((2, WIDE + AUX, WIDE), BF16),
            ((SPAN, WIDE), F32),
            ((SPAN, WIDE), BF16),
            ((SPAN, SPAN), BF16),
            ((SPAN, 2 * TOK), BF16),
            ((AUX, TOK), F32),
        ],
        where, decay_rates, got,
        scratch=[pltpu.VMEM((SPAN, WIDE), BF16), pltpu.VMEM((2, SPAN, WIDE), BF16)],
    )
    e1 = lax.ppermute(e, "z", [(i, i + 1) for i in range(3)])
    e2 = lax.ppermute(e, "z", [(i, i + 2) for i in range(2)])
    base, cm = call(
        inside_kernel,
        [SM, SM, VM, VM, VM, VM, VM],
        [((SPAN, WIDE), F32), ((SPAN, 2 * WIDE), BF16)],
        where, direct_weight, got, f, xs, m, fm,
        scratch=[pltpu.VMEM((SPAN, WIDE), BF16), pltpu.VMEM((SPAN, WIDE), BF16)],
    )
    (out,) = call(
        carry_kernel,
        [VM] * 6,
        [((PEERS, TOK, WIDE), BF16)],
        base, f, cm, e1, e2, meta,
        scratch=[pltpu.VMEM((2 * WIDE, WIDE), BF16)],
    )
    back = lax.all_to_all(out, ("dp", "y"), split_axis=0, concat_axis=0, tiled=True)
    (s0,) = call(square_kernel, [VM], [((AUX, TOK), F32)], back)
    others = [lax.ppermute(s0, "tensor", [(i, (i + k) % 4) for i in range(4)]) for k in (1, 2, 3)]

    def scale(*refs):
        scale_kernel(*refs, features=128 * 64)

    (mixed,) = call(scale, [VM] * 6, [((TOK, PEERS * WIDE), BF16)], back, s0, *others, norm_gain[None])
    return mixed[None]


def solution(mesh):
    fine = Mesh(mesh.devices.reshape(2, 4, 4, 4), ("dp", "z", "y", "tensor"))
    rows = ("z", "y")
    return jax.shard_map(
        per_device,
        mesh=fine,
        in_specs=(
            P("dp", rows, "tensor"),
            P("dp", rows, None, "tensor"),
            P("dp", rows, "tensor"),
            P("tensor"),
            P("tensor"),
            P("tensor"),
            P("dp", rows, None),
            P("dp", rows),
        ),
        out_specs=P("dp", rows, "tensor"),
        check_vma=False,
    )
```

```python
import jax
import jax.numpy as jnp
from jax import lax
from jax.experimental import pallas as pl
from jax.experimental.pallas import tpu as pltpu
from jax.sharding import Mesh, PartitionSpec as P


EPSILON = 1e-05
F32 = jnp.float32
BF16 = jnp.bfloat16
HIGH = lax.Precision.HIGHEST
TOK = 128
PEERS = 8
SPAN = TOK * PEERS
WIDE = 256
AUX = 8


def dot(a, b, dims, precision=None):
    return lax.dot_general(a, b, (dims, ((), ())), precision=precision, preferred_element_type=F32)


def iota(shape, dim):
    return lax.broadcasted_iota(jnp.int32, shape, dim)


def ones_where(cond, dtype=F32):
    return jnp.where(cond, 1.0, 0.0).astype(dtype)


def pack_kernel(
    tok_ref, bc_ref, dt_ref, route_ref, seg_ref, out_ref, c_ref, bc_buf, dt_buf, route_buf, seg_buf, sems
):
    small = ((route_ref, route_buf), (dt_ref, dt_buf), (seg_ref, seg_buf), (bc_ref, bc_buf))
    copies = [pltpu.make_async_copy(a, b, sems.at[n]) for n, (a, b) in enumerate(small)]
    for o in range(PEERS):
        src = tok_ref.at[:, o * WIDE : (o + 1) * WIDE]
        copies.append(pltpu.make_async_copy(src, out_ref.at[o, 0:TOK, 0:WIDE], sems.at[4 + o]))
    for copy in copies:
        copy.start()
    for copy in copies[:3]:
        copy.wait()
    block_of = ones_where(iota((16, TOK), 1) // 8 == iota((16, TOK), 0), BF16)
    spread = dot(dt_buf[...], block_of, ((0,), (0,)))
    same_u = iota((256, TOK), 0) % 8 == iota((256, TOK), 1) % 8
    spread = jnp.where(same_u, spread, 0.0).astype(BF16)
    head_of = ones_where(iota((32, 256), 1) // 8 == iota((32, 256), 0), BF16)
    dt_rows = dot(head_of, spread, ((1,), (0,)))
    route = jnp.broadcast_to(route_buf[...].astype(F32), (TOK, 16)).astype(BF16)
    route_row = dot(route, block_of, ((1,), (0,)))
    route_col = dot(block_of, route, ((0,), (1,)))
    ahead = (route_row == route_col) & (iota((TOK, TOK), 0) < iota((TOK, TOK), 1))
    place = jnp.sum(ones_where(ahead), axis=0, keepdims=True) + (lax.axis_index("dp") * TOK).astype(F32)
    segs = seg_buf[...]
    lane = iota((1, TOK), 1)
    starts = jnp.zeros((1, TOK), F32)
    for k in range(3):
        starts = jnp.where(lane == k, jnp.sum(ones_where(segs < k + 1), axis=1, keepdims=True), starts)
    row = iota((AUX, TOK), 0)
    for o in range(PEERS):
        aux = jnp.where(row == 4, route_row[0:1], jnp.where(row == 5, place, starts))
        for h in range(4):
            aux = jnp.where(row == h, dt_rows[o * 4 + h : o * 4 + h + 1], aux)
        out_ref[o, TOK : TOK + AUX, :] = jnp.concatenate([aux.astype(BF16)] * 4, axis=1)
    copies[3].wait()
    for g in range(2):
        b = bc_buf[:, 0, g * WIDE : (g + 1) * WIDE]
        c = bc_buf[:, 1, g * WIDE : (g + 1) * WIDE]
        for o in range(g * 4, g * 4 + 4):
            out_ref[o, :TOK, WIDE : 2 * WIDE] = b
            c_ref[o] = c
    for copy in copies[4:]:
        copy.wait()


def rate_lanes(ref):
    lane = iota((1, WIDE), 1) // 64
    first = (lax.axis_index("dp") * 4 + lax.axis_index("y")) * 4
    out = jnp.full((1, WIDE), ref[first], F32)
    for h in range(1, 4):
        out = jnp.where(lane == h, ref[first + h], out)
    return out


def keys_of(r_ref):
    pick_route = ones_where(iota((AUX, TOK), 0) == 4, BF16)
    pick_place = ones_where(iota((AUX, TOK), 0) == 5, BF16)
    starts = [[None] * 3, [None] * 3]
    rows, cols = [], []
    for q in range(PEERS):
        y, j = q // 2, q % 2
        aux = r_ref[j * 4 + y, TOK : TOK + AUX, 0:TOK]
        auxf = aux.astype(F32)
        rows.append((auxf[4:5], auxf[5:6] + y * 256.0))
        cols.append((dot(aux, pick_route, ((0,), (0,))), dot(aux, pick_place, ((0,), (0,))) + y * 256.0))
        for k in range(3):
            n = auxf[6:7, k : k + 1]
            starts[j][k] = n if starts[j][k] is None else starts[j][k] + n

    def key_of(route, place):
        second = route > 0.5
        doc = 4.0 * route
        for k in range(3):
            doc = doc + ones_where(place >= jnp.where(second, starts[1][k], starts[0][k]))
        return doc

    first, last = [], []
    for d in range(2):
        first.append(sum(ones_where(starts[d][k] <= 0.0) for k in range(3)))
        last.append(sum(ones_where(starts[d][k] <= SPAN - 1.0) for k in range(3)))
    return [key_of(*p) for p in rows], [key_of(*p) for p in cols], first, last


def state_kernel(rate_ref, r_ref, e_ref, f_ref, xs_ref, m_ref, dt_ref, bm_ref):
    rate = rate_lanes(rate_ref)
    spread = ones_where(iota((AUX, WIDE), 1) // 64 == iota((AUX, WIDE), 0), BF16)
    key_rows, key_cols, _, last = keys_of(r_ref)
    causal = iota((TOK, TOK), 0) >= iota((TOK, TOK), 1)
    for i in range(PEERS):
        src = (i % 2) * 4 + i // 2
        dt_ref[i * TOK : (i + 1) * TOK, :] = dot(r_ref[src, TOK : TOK + AUX, 0:TOK], spread, ((0,), (0,))).astype(BF16)
        for jj in range(i + 1 + (i + 1) % 2):
            if jj > i:
                m = jnp.zeros((TOK, TOK), BF16)
            else:
                same = key_cols[i] == key_rows[jj]
                m = ones_where(same & causal if i == jj else same, BF16)
            m_ref[i * TOK : (i + 1) * TOK, jj * TOK : (jj + 1) * TOK] = m
        for d in range(2):
            lm = ones_where(key_cols[i] == last[d] + 4.0 * d, BF16)
            for half in range(2):
                bm_ref[d, i * TOK : (i + 1) * TOK, half * TOK : (half + 1) * TOK] = (
                    r_ref[src, :TOK, WIDE + half * TOK : WIDE + (half + 1) * TOK] * lm
                )
    for b in range(4):
        sl = slice(b * 256, (b + 1) * 256)
        total = dot(m_ref[sl, : (b + 1) * 256], dt_ref[: (b + 1) * 256, :], ((1,), (0,)))
        f_ref[sl, :] = jnp.exp(-rate * total)
        grow = jnp.exp(rate * total) * dt_ref[sl, :].astype(F32)
        for s in range(2):
            x = r_ref[s * 4 + b, :TOK, 0:WIDE].astype(F32)
            at = b * 256 + s * TOK
            xs_ref[at : at + TOK, :] = (x * grow[s * TOK : (s + 1) * TOK]).astype(BF16)
    row8 = iota((AUX, WIDE), 0)
    for d in range(2):
        total = jnp.zeros((AUX, WIDE), F32)
        for q in range(PEERS):
            lm = jnp.broadcast_to(ones_where(key_rows[q] == last[d] + 4.0 * d), (AUX, TOK)).astype(BF16)
            total = total + dot(lm, dt_ref[q * TOK : (q + 1) * TOK, :], ((1,), (0,)))
        through = jnp.exp(-rate * total)
        e = dot(bm_ref[d], xs_ref[...], ((0,), (0,))) * through[0:1]
        e_ref[d, 0:WIDE, :] = e.astype(BF16)
        e_ref[d, WIDE : WIDE + AUX, :] = jnp.where(row8 == 0, through, last[d]).astype(BF16)


def inside_kernel(weight_ref, r_ref, got_ref, f_ref, xs_ref, base_ref, cm_ref, meta_ref, b_ref, c_ref):
    weight = rate_lanes(weight_ref)
    key_rows, key_cols, first, _ = keys_of(r_ref)
    meta_ref[...] = jnp.where(iota((AUX, TOK), 0) == 0, first[0], first[1])
    for q in range(PEERS):
        src = (q % 2) * 4 + q // 2
        sl = slice(q * TOK, (q + 1) * TOK)
        b_ref[sl, :] = r_ref[src, :TOK, WIDE : 2 * WIDE]
        c = got_ref[src]
        c_ref[sl, :] = c
        for d in range(2):
            fm = ones_where(key_cols[q] == first[d] + 4.0 * d, BF16)
            for half in range(2):
                at = d * WIDE + half * TOK
                cm_ref[sl, at : at + TOK] = c[:, half * TOK : (half + 1) * TOK] * fm
    causal = iota((256, 256), 0) >= iota((256, 256), 1)
    for i in range(4):
        si = slice(i * 256, (i + 1) * 256)
        acc = jnp.zeros((256, WIDE), F32)
        keys = jnp.concatenate([jnp.concatenate([key_cols[2 * i + n]] * 2, axis=1) for n in range(2)], axis=0)
        for j in range(i + 1):
            sj = slice(j * 256, (j + 1) * 256)
            s = dot(c_ref[si, :], b_ref[sj, :], ((1,), (1,)))
            same = keys == jnp.concatenate(key_rows[2 * j : 2 * j + 2], axis=1)
            w = jnp.where(same & causal if i == j else same, s, 0.0).astype(BF16)
            acc = acc + dot(w, xs_ref[sj, :], ((1,), (0,)))
        acc = acc * f_ref[si, :]
        for s in range(2):
            x = r_ref[s * 4 + i, :TOK, 0:WIDE].astype(F32)
            at = i * 256 + s * TOK
            base_ref[at : at + TOK, :] = acc[s * TOK : (s + 1) * TOK] + weight * x


def carry_kernel(base_ref, f_ref, cm_ref, e1_ref, e2_ref, meta_ref, y_ref, h_ref):
    for d in range(2):
        first = meta_ref[d : d + 1, 0:1]
        joined1 = e1_ref[d, WIDE + 1 : WIDE + 2, :].astype(F32) == first
        joined2 = joined1 & (e2_ref[d, WIDE + 1 : WIDE + 2, :].astype(F32) == first)
        through = jnp.where(joined2, e1_ref[d, WIDE : WIDE + 1, :].astype(F32), 0.0)
        near = jnp.where(joined1, e1_ref[d, 0:WIDE, :].astype(F32), 0.0)
        h_ref[d * WIDE : (d + 1) * WIDE, :] = (near + through * e2_ref[d, 0:WIDE, :].astype(F32)).astype(BF16)
    for q in range(PEERS):
        sl = slice(q * TOK, (q + 1) * TOK)
        y = base_ref[sl, :] + f_ref[sl, :] * dot(cm_ref[sl, :], h_ref[...], ((1,), (0,)))
        y_ref[(q % 2) * 4 + q // 2] = y.astype(BF16)


def square_kernel(y_ref, s_ref):
    acc = jnp.zeros((TOK, WIDE), F32)
    for o in range(PEERS):
        v = y_ref[o].astype(F32)
        acc = acc + v * v
    s_ref[...] = dot(jnp.ones((AUX, WIDE), F32), acc, ((1,), (1,)), HIGH)


def scale_kernel(y_ref, s0_ref, s1_ref, s2_ref, s3_ref, gain_ref, out_ref, *, features):
    total = (s0_ref[...] + s1_ref[...]) + (s2_ref[...] + s3_ref[...])
    pick = ones_where(iota((AUX, TOK), 0) == 0)
    col = dot(total, pick, ((0,), (0,)), HIGH)
    scale = lax.rsqrt(col / features + EPSILON)
    scale = jnp.concatenate([scale, scale], axis=1)
    for o in range(PEERS):
        sl = slice(o * WIDE, (o + 1) * WIDE)
        out_ref[:, sl] = (y_ref[o].astype(F32) * scale * gain_ref[:, sl]).astype(BF16)


VM = pl.BlockSpec(memory_space=pltpu.VMEM)
SM = pl.BlockSpec(memory_space=pltpu.SMEM)
HB = pl.BlockSpec(memory_space=pl.ANY)


def kept(x):
    return pltpu.with_memory_space_constraint(x, pltpu.VMEM)


def far(x):
    return pltpu.with_memory_space_constraint(x, pltpu.HBM)


def call(kernel, specs, outs, *args, scratch=()):
    return pl.pallas_call(
        kernel,
        in_specs=specs,
        out_specs=[VM] * len(outs),
        out_shape=outs,
        scratch_shapes=list(scratch),
        compiler_params=pltpu.CompilerParams(vmem_limit_bytes=14 << 20),
    )(*args)


def whole(tokens, bc_proj, step_sizes, decay_rates, direct_weight, norm_gain, routes, segments):
    V = pltpu.VMEM
    send, send_c = call(
        pack_kernel,
        [HB] * 5,
        [V((PEERS, TOK + AUX, 2 * WIDE), BF16), V((PEERS, TOK, WIDE), BF16)],
        far(tokens[0]), far(bc_proj[0]), far(step_sizes[0]), far(routes.reshape(1, 16)), far(segments),
        scratch=[
            V((TOK, 2, 2 * WIDE), BF16),
            V((16, 256), BF16),
            V((1, 16), jnp.int32),
            V((1, 256), jnp.int32),
            pltpu.SemaphoreType.DMA((4 + PEERS,)),
        ],
    )
    got = kept(lax.all_to_all(send, ("dp", "y"), split_axis=0, concat_axis=0, tiled=True))
    got_c = kept(lax.all_to_all(send_c, ("dp", "y"), split_axis=0, concat_axis=0, tiled=True))
    e, f, xs = call(
        state_kernel,
        [SM, VM],
        [pltpu.HBM((2, WIDE + AUX, WIDE), BF16), V((SPAN, WIDE), F32), V((SPAN, WIDE), BF16)],
        decay_rates, got,
        scratch=[V((SPAN, SPAN), BF16), V((SPAN, WIDE), BF16), V((2, SPAN, WIDE), BF16)],
    )
    f, xs = kept(f), kept(xs)
    e2 = kept(lax.ppermute(e, "z", [(i, i + 2) for i in range(2)]))
    e1 = kept(lax.ppermute(e, "z", [(i, i + 1) for i in range(3)]))
    base, cm, meta = call(
        inside_kernel,
        [SM] + [VM] * 4,
        [V((SPAN, WIDE), F32), V((SPAN, 2 * WIDE), BF16), V((AUX, TOK), F32)],
        direct_weight, got, got_c, f, xs,
        scratch=[V((SPAN, WIDE), BF16), V((SPAN, WIDE), BF16)],
    )
    (out,) = call(
        carry_kernel,
        [VM] * 6,
        [V((PEERS, TOK, WIDE), BF16)],
        kept(base), f, kept(cm), e1, e2, kept(meta),
        scratch=[V((2 * WIDE, WIDE), BF16)],
    )
    back = kept(lax.all_to_all(out, ("dp", "y"), split_axis=0, concat_axis=0, tiled=True))
    (s0,) = call(square_kernel, [VM], [V((AUX, TOK), F32)], back)
    others = [kept(lax.ppermute(s0, "tensor", [(i, (i + k) % 4) for i in range(4)])) for k in (1, 2, 3)]

    def scale(*refs):
        scale_kernel(*refs, features=128 * 64)

    out_shape = [jax.ShapeDtypeStruct((TOK, PEERS * WIDE), BF16)]
    (mixed,) = call(scale, [VM] * 6, out_shape, back, kept(s0), *others, norm_gain[None])
    return mixed[None]


def solution(mesh):
    fine = Mesh(mesh.devices.reshape(2, 4, 4, 4), ("dp", "z", "y", "tensor"))
    rows = ("z", "y")
    return jax.shard_map(
        whole,
        mesh=fine,
        in_specs=(
            P("dp", rows, "tensor"),
            P("dp", rows, None, "tensor"),
            P("dp", rows, "tensor"),
            P("tensor"),
            P("tensor"),
            P("tensor"),
            P("dp", rows, None),
            P("dp", rows),
        ),
        out_specs=P("dp", rows, "tensor"),
        check_vma=False,
    )
```

```python
import jax
import jax.numpy as jnp
from jax import lax
from jax.experimental import pallas as pl
from jax.experimental.pallas import tpu as pltpu
from jax.sharding import Mesh, PartitionSpec as P


EPSILON = 1e-05
F32 = jnp.float32
BF16 = jnp.bfloat16
HIGH = lax.Precision.HIGHEST
TOK = 128
PEERS = 8
SPAN = TOK * PEERS
WIDE = 256
AUX = 8


def dot(a, b, dims, precision=None):
    return lax.dot_general(a, b, (dims, ((), ())), precision=precision, preferred_element_type=F32)


def iota(shape, dim):
    return lax.broadcasted_iota(jnp.int32, shape, dim)


def ones_where(cond, dtype=F32):
    return jnp.where(cond, 1.0, 0.0).astype(dtype)


def pack_kernel(
    tok_ref, bc_ref, dt_ref, route_ref, seg_ref, out_ref, c_ref, bc_buf, dt_buf, route_buf, seg_buf, sems
):
    small = ((route_ref, route_buf), (dt_ref, dt_buf), (seg_ref, seg_buf), (bc_ref, bc_buf))
    copies = [pltpu.make_async_copy(a, b, sems.at[n]) for n, (a, b) in enumerate(small)]
    for o in range(PEERS):
        src = tok_ref.at[:, o * WIDE : (o + 1) * WIDE]
        copies.append(pltpu.make_async_copy(src, out_ref.at[o, 0:TOK, 0:WIDE], sems.at[4 + o]))
    for copy in copies:
        copy.start()
    for copy in copies[:3]:
        copy.wait()
    block_of = ones_where(iota((16, TOK), 1) // 8 == iota((16, TOK), 0), BF16)
    spread = dot(dt_buf[...], block_of, ((0,), (0,)))
    same_u = iota((256, TOK), 0) % 8 == iota((256, TOK), 1) % 8
    spread = jnp.where(same_u, spread, 0.0).astype(BF16)
    head_of = ones_where(iota((32, 256), 1) // 8 == iota((32, 256), 0), BF16)
    dt_rows = dot(head_of, spread, ((1,), (0,)))
    route = jnp.broadcast_to(route_buf[...].astype(F32), (TOK, 16)).astype(BF16)
    route_row = dot(route, block_of, ((1,), (0,)))
    route_col = dot(block_of, route, ((0,), (1,)))
    ahead = (route_row == route_col) & (iota((TOK, TOK), 0) < iota((TOK, TOK), 1))
    place = jnp.sum(ones_where(ahead), axis=0, keepdims=True) + (lax.axis_index("dp") * TOK).astype(F32)
    segs = seg_buf[...]
    lane = iota((1, TOK), 1)
    starts = jnp.zeros((1, TOK), F32)
    for k in range(3):
        starts = jnp.where(lane == k, jnp.sum(ones_where(segs < k + 1), axis=1, keepdims=True), starts)
    row = iota((AUX, TOK), 0)
    for o in range(PEERS):
        aux = jnp.where(row == 4, route_row[0:1], jnp.where(row == 5, place, starts))
        for h in range(4):
            aux = jnp.where(row == h, dt_rows[o * 4 + h : o * 4 + h + 1], aux)
        out_ref[o, TOK : TOK + AUX, :] = jnp.concatenate([aux.astype(BF16)] * 4, axis=1)
    copies[3].wait()
    for g in range(2):
        b = bc_buf[:, 0, g * WIDE : (g + 1) * WIDE]
        c = bc_buf[:, 1, g * WIDE : (g + 1) * WIDE]
        for o in range(g * 4, g * 4 + 4):
            out_ref[o, :TOK, WIDE : 2 * WIDE] = b
            c_ref[o] = c
    for copy in copies[4:]:
        copy.wait()


def rate_lanes(ref):
    lane = iota((1, WIDE), 1) // 64
    first = (lax.axis_index("dp") * 4 + lax.axis_index("y")) * 4
    out = jnp.full((1, WIDE), ref[first], F32)
    for h in range(1, 4):
        out = jnp.where(lane == h, ref[first + h], out)
    return out


def keys_of(r_ref):
    pick_route = ones_where(iota((AUX, TOK), 0) == 4, BF16)
    pick_place = ones_where(iota((AUX, TOK), 0) == 5, BF16)
    starts = [[None] * 3, [None] * 3]
    rows, cols = [], []
    for q in range(PEERS):
        y, j = q // 2, q % 2
        aux = r_ref[j * 4 + y, TOK : TOK + AUX, 0:TOK]
        auxf = aux.astype(F32)
        rows.append((auxf[4:5], auxf[5:6] + y * 256.0))
        cols.append((dot(aux, pick_route, ((0,), (0,))), dot(aux, pick_place, ((0,), (0,))) + y * 256.0))
        for k in range(3):
            n = auxf[6:7, k : k + 1]
            starts[j][k] = n if starts[j][k] is None else starts[j][k] + n

    def key_of(route, place):
        second = route > 0.5
        doc = 4.0 * route
        for k in range(3):
            doc = doc + ones_where(place >= jnp.where(second, starts[1][k], starts[0][k]))
        return doc

    first, last = [], []
    for d in range(2):
        first.append(sum(ones_where(starts[d][k] <= 0.0) for k in range(3)))
        last.append(sum(ones_where(starts[d][k] <= SPAN - 1.0) for k in range(3)))
    return [key_of(*p) for p in rows], [key_of(*p) for p in cols], first, last


def state_kernel(rate_ref, r_ref, e_ref, f_ref, xs_ref, own_ref, m_ref, dt_ref, bm_ref):
    rate = rate_lanes(rate_ref)
    spread = ones_where(iota((AUX, WIDE), 1) // 64 == iota((AUX, WIDE), 0), BF16)
    key_rows, key_cols, first, last = keys_of(r_ref)
    causal = iota((TOK, TOK), 0) >= iota((TOK, TOK), 1)
    for i in range(PEERS):
        src = (i % 2) * 4 + i // 2
        dt_ref[i * TOK : (i + 1) * TOK, :] = dot(r_ref[src, TOK : TOK + AUX, 0:TOK], spread, ((0,), (0,))).astype(BF16)
        for jj in range(i + 1 + (i + 1) % 2):
            if jj > i:
                m = jnp.zeros((TOK, TOK), BF16)
            else:
                same = key_cols[i] == key_rows[jj]
                m = ones_where(same & causal if i == jj else same, BF16)
            m_ref[i * TOK : (i + 1) * TOK, jj * TOK : (jj + 1) * TOK] = m
        for d in range(2):
            lm = ones_where(key_cols[i] == last[d] + 4.0 * d, BF16)
            for half in range(2):
                bm_ref[d, i * TOK : (i + 1) * TOK, half * TOK : (half + 1) * TOK] = (
                    r_ref[src, :TOK, WIDE + half * TOK : WIDE + (half + 1) * TOK] * lm
                )
    for b in range(4):
        sl = slice(b * 256, (b + 1) * 256)
        total = dot(m_ref[sl, : (b + 1) * 256], dt_ref[: (b + 1) * 256, :], ((1,), (0,)))
        f_ref[sl, :] = jnp.exp(-rate * total)
        grow = jnp.exp(rate * total) * dt_ref[sl, :].astype(F32)
        for s in range(2):
            x = r_ref[s * 4 + b, :TOK, 0:WIDE].astype(F32)
            at = b * 256 + s * TOK
            xs_ref[at : at + TOK, :] = (x * grow[s * TOK : (s + 1) * TOK]).astype(BF16)
    row8 = iota((AUX, WIDE), 0)
    for d in range(2):
        total = jnp.zeros((AUX, WIDE), F32)
        for q in range(PEERS):
            lm = jnp.broadcast_to(ones_where(key_rows[q] == last[d] + 4.0 * d), (AUX, TOK)).astype(BF16)
            total = total + dot(lm, dt_ref[q * TOK : (q + 1) * TOK, :], ((1,), (0,)))
        through = jnp.exp(-rate * total)
        e = dot(bm_ref[d], xs_ref[...], ((0,), (0,))) * through[0:1]
        e_ref[d, 0:WIDE, :] = e.astype(BF16)
        e_ref[d, WIDE : WIDE + AUX, :] = jnp.broadcast_to(last[d], (AUX, WIDE)).astype(BF16)
        own_ref[d] = jnp.where(row8 == 0, jnp.where(first[d] == last[d], through, 0.0), first[d])


def inside_kernel(weight_ref, r_ref, got_ref, f_ref, xs_ref, base_ref, cm_ref, b_ref, c_ref):
    weight = rate_lanes(weight_ref)
    key_rows, key_cols, first, _ = keys_of(r_ref)
    for q in range(PEERS):
        src = (q % 2) * 4 + q // 2
        sl = slice(q * TOK, (q + 1) * TOK)
        b_ref[sl, :] = r_ref[src, :TOK, WIDE : 2 * WIDE]
        c = got_ref[src]
        c_ref[sl, :] = c
        for d in range(2):
            fm = ones_where(key_cols[q] == first[d] + 4.0 * d, BF16)
            for half in range(2):
                at = d * WIDE + half * TOK
                cm_ref[sl, at : at + TOK] = c[:, half * TOK : (half + 1) * TOK] * fm
    causal = iota((256, 256), 0) >= iota((256, 256), 1)
    for i in range(4):
        si = slice(i * 256, (i + 1) * 256)
        acc = jnp.zeros((256, WIDE), F32)
        keys = jnp.concatenate([jnp.concatenate([key_cols[2 * i + n]] * 2, axis=1) for n in range(2)], axis=0)
        for j in range(i + 1):
            sj = slice(j * 256, (j + 1) * 256)
            s = dot(c_ref[si, :], b_ref[sj, :], ((1,), (1,)))
            same = keys == jnp.concatenate(key_rows[2 * j : 2 * j + 2], axis=1)
            w = jnp.where(same & causal if i == j else same, s, 0.0).astype(BF16)
            acc = acc + dot(w, xs_ref[sj, :], ((1,), (0,)))
        acc = acc * f_ref[si, :]
        for s in range(2):
            x = r_ref[s * 4 + i, :TOK, 0:WIDE].astype(F32)
            at = i * 256 + s * TOK
            base_ref[at : at + TOK, :] = acc[s * TOK : (s + 1) * TOK] + weight * x


def pass_kernel(e_ref, own_ref, out_ref):
    for d in range(2):
        joined = e_ref[d, WIDE : WIDE + 1, :].astype(F32) == own_ref[d, 1:2, :]
        through = jnp.where(joined, own_ref[d, 0:1, :], 0.0)
        out_ref[d] = (through * e_ref[d, 0:WIDE, :].astype(F32)).astype(BF16)


def carry_kernel(base_ref, f_ref, cm_ref, e1_ref, e2_ref, own_ref, y_ref, h_ref):
    for d in range(2):
        joined = e1_ref[d, WIDE : WIDE + 1, :].astype(F32) == own_ref[d, 1:2, :]
        h = e1_ref[d, 0:WIDE, :].astype(F32) + e2_ref[d].astype(F32)
        h_ref[d * WIDE : (d + 1) * WIDE, :] = jnp.where(joined, h, 0.0).astype(BF16)
    for q in range(PEERS):
        sl = slice(q * TOK, (q + 1) * TOK)
        y = base_ref[sl, :] + f_ref[sl, :] * dot(cm_ref[sl, :], h_ref[...], ((1,), (0,)))
        y_ref[(q % 2) * 4 + q // 2] = y.astype(BF16)


def square_kernel(y_ref, s_ref):
    acc = jnp.zeros((TOK, WIDE), F32)
    for o in range(PEERS):
        v = y_ref[o].astype(F32)
        acc = acc + v * v
    s_ref[...] = dot(jnp.ones((AUX, WIDE), F32), acc, ((1,), (1,)), HIGH)


def scale_kernel(y_ref, s0_ref, s1_ref, s2_ref, s3_ref, gain_ref, out_ref, *, features):
    total = (s0_ref[...] + s1_ref[...]) + (s2_ref[...] + s3_ref[...])
    pick = ones_where(iota((AUX, TOK), 0) == 0)
    col = dot(total, pick, ((0,), (0,)), HIGH)
    scale = lax.rsqrt(col / features + EPSILON)
    scale = jnp.concatenate([scale, scale], axis=1)
    for o in range(PEERS):
        sl = slice(o * WIDE, (o + 1) * WIDE)
        out_ref[:, sl] = (y_ref[o].astype(F32) * scale * gain_ref[:, sl]).astype(BF16)


VM = pl.BlockSpec(memory_space=pltpu.VMEM)
SM = pl.BlockSpec(memory_space=pltpu.SMEM)
HB = pl.BlockSpec(memory_space=pl.ANY)


def kept(x):
    return pltpu.with_memory_space_constraint(x, pltpu.VMEM)


def far(x):
    return pltpu.with_memory_space_constraint(x, pltpu.HBM)


def call(kernel, specs, outs, *args, scratch=()):
    return pl.pallas_call(
        kernel,
        in_specs=specs,
        out_specs=[VM] * len(outs),
        out_shape=outs,
        scratch_shapes=list(scratch),
        compiler_params=pltpu.CompilerParams(vmem_limit_bytes=14 << 20),
    )(*args)


def whole(tokens, bc_proj, step_sizes, decay_rates, direct_weight, norm_gain, routes, segments):
    V = pltpu.VMEM
    send, send_c = call(
        pack_kernel,
        [HB] * 5,
        [V((PEERS, TOK + AUX, 2 * WIDE), BF16), pltpu.HBM((PEERS, TOK, WIDE), BF16)],
        far(tokens[0]), far(bc_proj[0]), far(step_sizes[0]), far(routes.reshape(1, 16)), far(segments),
        scratch=[
            V((TOK, 2, 2 * WIDE), BF16),
            V((16, 256), BF16),
            V((1, 16), jnp.int32),
            V((1, 256), jnp.int32),
            pltpu.SemaphoreType.DMA((4 + PEERS,)),
        ],
    )
    got = kept(lax.all_to_all(send, ("dp", "y"), split_axis=0, concat_axis=0, tiled=True))
    e, f, xs, own = call(
        state_kernel,
        [SM, VM],
        [pltpu.HBM((2, WIDE + AUX, WIDE), BF16), V((SPAN, WIDE), F32), V((SPAN, WIDE), BF16), V((2, AUX, WIDE), F32)],
        decay_rates, got,
        scratch=[V((SPAN, SPAN), BF16), V((SPAN, WIDE), BF16), V((2, SPAN, WIDE), BF16)],
    )
    f, xs, own = kept(f), kept(xs), kept(own)
    e, send_c = lax.optimization_barrier((e, send_c))
    e1 = kept(lax.ppermute(e, "z", [(i, i + 1) for i in range(3)]))
    got_c = kept(lax.all_to_all(send_c, ("dp", "y"), split_axis=0, concat_axis=0, tiled=True))
    (older,) = call(pass_kernel, [VM, VM], [pltpu.HBM((2, WIDE, WIDE), BF16)], e1, own)
    e2 = kept(lax.ppermute(older, "z", [(i, i + 1) for i in range(1, 3)]))
    base, cm = call(
        inside_kernel,
        [SM] + [VM] * 4,
        [V((SPAN, WIDE), F32), V((SPAN, 2 * WIDE), BF16)],
        direct_weight, got, got_c, f, xs,
        scratch=[V((SPAN, WIDE), BF16), V((SPAN, WIDE), BF16)],
    )
    (out,) = call(
        carry_kernel,
        [VM] * 6,
        [V((PEERS, TOK, WIDE), BF16)],
        kept(base), f, kept(cm), e1, e2, own,
        scratch=[V((2 * WIDE, WIDE), BF16)],
    )
    back = kept(lax.all_to_all(out, ("dp", "y"), split_axis=0, concat_axis=0, tiled=True))
    (s0,) = call(square_kernel, [VM], [V((AUX, TOK), F32)], back)
    others = [kept(lax.ppermute(s0, "tensor", [(i, (i + k) % 4) for i in range(4)])) for k in (1, 2, 3)]

    def scale(*refs):
        scale_kernel(*refs, features=128 * 64)

    out_shape = [jax.ShapeDtypeStruct((TOK, PEERS * WIDE), BF16)]
    (mixed,) = call(scale, [VM] * 6, out_shape, back, kept(s0), *others, norm_gain[None])
    return mixed[None]


def solution(mesh):
    fine = Mesh(mesh.devices.reshape(2, 4, 4, 4), ("dp", "z", "y", "tensor"))
    rows = ("z", "y")
    return jax.shard_map(
        whole,
        mesh=fine,
        in_specs=(
            P("dp", rows, "tensor"),
            P("dp", rows, None, "tensor"),
            P("dp", rows, "tensor"),
            P("tensor"),
            P("tensor"),
            P("tensor"),
            P("dp", rows, None),
            P("dp", rows),
        ),
        out_specs=P("dp", rows, "tensor"),
        check_vma=False,
    )
```

```python
import jax
import jax.numpy as jnp
from jax import lax
from jax.experimental import pallas as pl
from jax.experimental.pallas import tpu as pltpu
from jax.sharding import Mesh, PartitionSpec as P


EPSILON = 1e-05
F32 = jnp.float32
BF16 = jnp.bfloat16
HIGH = lax.Precision.HIGHEST
TOK = 128
PEERS = 8
SPAN = TOK * PEERS
WIDE = 256
AUX = 8


def dot(a, b, dims, precision=None):
    return lax.dot_general(a, b, (dims, ((), ())), precision=precision, preferred_element_type=F32)


def iota(shape, dim):
    return lax.broadcasted_iota(jnp.int32, shape, dim)


def ones_where(cond, dtype=F32):
    return jnp.where(cond, 1.0, 0.0).astype(dtype)


def pack_kernel(
    tok_ref, bc_ref, dt_ref, route_ref, seg_ref, out_ref, c_ref, bc_buf, dt_buf, route_buf, seg_buf, wide_ref, sems
):
    small = ((route_ref, route_buf), (dt_ref, dt_buf), (seg_ref, seg_buf), (bc_ref, bc_buf))
    copies = [pltpu.make_async_copy(a, b, sems.at[n]) for n, (a, b) in enumerate(small)]
    for o in range(PEERS):
        src = tok_ref.at[:, o * WIDE : (o + 1) * WIDE]
        copies.append(pltpu.make_async_copy(src, out_ref.at[o, 0:TOK, 0:WIDE], sems.at[4 + o]))
    for copy in copies:
        copy.start()
    for copy in copies[:3]:
        copy.wait()
    block_of = ones_where(iota((16, TOK), 1) // 8 == iota((16, TOK), 0), BF16)
    spread = dot(dt_buf[...], block_of, ((0,), (0,)))
    same_u = iota((256, TOK), 0) % 8 == iota((256, TOK), 1) % 8
    spread = jnp.where(same_u, spread, 0.0).astype(BF16)
    head_of = ones_where(iota((32, 256), 1) // 8 == iota((32, 256), 0), BF16)
    dt_rows = dot(head_of, spread, ((1,), (0,)))
    route = jnp.broadcast_to(route_buf[...].astype(F32), (TOK, 16)).astype(BF16)
    route_row = dot(route, block_of, ((1,), (0,)))
    route_col = dot(block_of, route, ((0,), (1,)))
    ahead = (route_row == route_col) & (iota((TOK, TOK), 0) < iota((TOK, TOK), 1))
    place = jnp.sum(ones_where(ahead), axis=0, keepdims=True) + (lax.axis_index("dp") * TOK).astype(F32)
    segs = seg_buf[...]
    lane = iota((1, TOK), 1)
    starts = jnp.zeros((1, TOK), F32)
    for k in range(3):
        starts = jnp.where(lane == k, jnp.sum(ones_where(segs < k + 1), axis=1, keepdims=True), starts)
    row = iota((AUX, TOK), 0)
    for o in range(PEERS):
        aux = jnp.where(row == 4, route_row[0:1], jnp.where(row == 5, place, starts))
        for h in range(4):
            aux = jnp.where(row == h, dt_rows[o * 4 + h : o * 4 + h + 1], aux)
        out_ref[o, TOK : TOK + AUX, :] = jnp.concatenate([aux.astype(BF16)] * 4, axis=1)
    copies[3].wait()
    wide_ref[...] = bc_buf[...].astype(F32)
    for tile in range(4):
        g, half = tile // 2, tile % 2
        b = wide_ref[pl.ds(2 * tile, TOK, stride=8), :].astype(BF16)
        c = wide_ref[pl.ds(2 * tile + 1, TOK, stride=8), :].astype(BF16)
        for o in range(g * 4, g * 4 + 4):
            out_ref[o, :TOK, WIDE + half * TOK : WIDE + (half + 1) * TOK] = b
            c_ref[o, :, half * TOK : (half + 1) * TOK] = c
    for copy in copies[4:]:
        copy.wait()


def rate_lanes(ref):
    lane = iota((1, WIDE), 1) // 64
    first = (lax.axis_index("dp") * 4 + lax.axis_index("y")) * 4
    out = jnp.full((1, WIDE), ref[first], F32)
    for h in range(1, 4):
        out = jnp.where(lane == h, ref[first + h], out)
    return out


def keys_of(r_ref):
    pick_route = ones_where(iota((AUX, TOK), 0) == 4, BF16)
    pick_place = ones_where(iota((AUX, TOK), 0) == 5, BF16)
    starts = [[None] * 3, [None] * 3]
    rows, cols = [], []
    for q in range(PEERS):
        y, j = q // 2, q % 2
        aux = r_ref[j * 4 + y, TOK : TOK + AUX, 0:TOK]
        auxf = aux.astype(F32)
        rows.append((auxf[4:5], auxf[5:6] + y * 256.0))
        cols.append((dot(aux, pick_route, ((0,), (0,))), dot(aux, pick_place, ((0,), (0,))) + y * 256.0))
        for k in range(3):
            n = auxf[6:7, k : k + 1]
            starts[j][k] = n if starts[j][k] is None else starts[j][k] + n

    def key_of(route, place):
        second = route > 0.5
        doc = 4.0 * route
        for k in range(3):
            doc = doc + ones_where(place >= jnp.where(second, starts[1][k], starts[0][k]))
        return doc

    first, last = [], []
    for d in range(2):
        first.append(sum(ones_where(starts[d][k] <= 0.0) for k in range(3)))
        last.append(sum(ones_where(starts[d][k] <= SPAN - 1.0) for k in range(3)))
    return [key_of(*p) for p in rows], [key_of(*p) for p in cols], first, last


def three(x, lane):
    top = x.astype(BF16).astype(F32)
    rest = x - top
    mid = rest.astype(BF16).astype(F32)
    return jnp.where(lane < 32, top, jnp.where(lane < 64, mid, jnp.where(lane < 96, rest - mid, 0.0))).astype(BF16)


def state_kernel(rate_ref, r_ref, e_ref, f_ref, xs_ref, own_ref, bt_ref):
    rate = rate_lanes(rate_ref)
    lane = iota((1, TOK), 1)
    key = lane % 32 // 4
    row, col = iota((AUX, TOK), 0), iota((AUX, TOK), 1)
    code_of = jnp.where(row == 5, 1.0, jnp.where(row == 4, 2048.0, 0.0)).astype(BF16)
    dt_of = ones_where(row == col % 4, BF16)
    spread = ones_where(iota((AUX, WIDE), 1) // 64 == iota((AUX, WIDE), 0), BF16)
    columns = jnp.concatenate([code_of, dt_of, spread], axis=1)
    expand = ones_where(iota((TOK, WIDE), 0) % 4 == iota((TOK, WIDE), 1) // 64, BF16)
    lower = ones_where(iota((256, 256), 0) >= iota((256, 256), 1), BF16)
    auxs = [r_ref[q % 2 * 4 + q // 2, TOK : TOK + AUX, 0:TOK] for q in range(PEERS)]
    auxf = [a.astype(F32) for a in auxs]
    starts = [[sum(auxf[2 * y + d][6:7, k : k + 1] for y in range(4)) for k in range(3)] for d in range(2)]
    first = [sum(ones_where(starts[d][k] <= 0.0) for k in range(3)) for d in range(2)]
    last = [sum(ones_where(starts[d][k] <= SPAN - 1.0) for k in range(3)) for d in range(2)]
    low, high = jnp.zeros((1, TOK), F32), jnp.zeros((1, TOK), F32)
    final = []
    for d in range(2):
        edges = [jnp.zeros((1, 1), F32)] + starts[d] + [jnp.full((1, 1), float(SPAN), F32)]
        at = edges[0]
        for n in range(4):
            low = jnp.where(key == 4 * d + n, edges[n] + 2048.0 * d, low)
            high = jnp.where(key == 4 * d + n, edges[n + 1] + 2048.0 * d, high)
            at = jnp.where(last[d] == n, edges[n], at)
        final.append(at + 2048.0 * d)
    for q in range(PEERS):
        code = auxf[q][4:5] * 2048.0 + auxf[q][5:6] + (q // 2) * 256.0
        bt = jnp.transpose(r_ref[q % 2 * 4 + q // 2, :TOK, WIDE : 2 * WIDE])
        for d in range(2):
            ends = jnp.broadcast_to(ones_where((code >= final[d]) & (code < 2048.0 * (d + 1))), (16, TOK)).astype(BF16)
            bt_ref[d, :, q * TOK : (q + 1) * TOK] = bt * ends[0:1]
    total = jnp.zeros((1, TOK), F32)
    for b in range(4):
        parts = [dot(auxs[2 * b + s], columns, ((0,), (0,))) for s in range(2)]
        part = jnp.concatenate(parts, axis=0)
        code = part[:, 0:TOK] + b * 256.0
        mine = (code >= low) & (code < high)
        z = jnp.where(mine, part[:, TOK : 2 * TOK], 0.0).astype(BF16)
        sums = dot(lower, z, ((1,), (0,))) + total
        total = sums[255:256]
        d_wide = dot(three(jnp.where(mine, sums, 0.0), lane), expand, ((1,), (0,)))
        f_ref[b * 256 : (b + 1) * 256, :] = jnp.exp(-rate * d_wide)
        grow = jnp.exp(rate * d_wide) * part[:, 2 * TOK :]
        for s in range(2):
            x = r_ref[s * 4 + b, :TOK, 0:WIDE].astype(F32)
            at = b * 256 + s * TOK
            xs_ref[at : at + TOK, :] = (x * grow[s * TOK : (s + 1) * TOK]).astype(BF16)
    row8 = iota((AUX, WIDE), 0)
    for d in range(2):
        tail = jnp.broadcast_to(jnp.where(key == last[d].astype(jnp.int32) + 4 * d, total, 0.0), (AUX, TOK))
        through = jnp.exp(-rate * dot(three(tail, lane), expand, ((1,), (0,))))
        e = dot(bt_ref[d], xs_ref[...], ((1,), (0,))) * through[0:1]
        e_ref[d, 0:WIDE, :] = e.astype(BF16)
        e_ref[d, WIDE : WIDE + AUX, :] = jnp.broadcast_to(last[d], (AUX, WIDE)).astype(BF16)
        own_ref[d] = jnp.where(row8 == 0, jnp.where(first[d] == last[d], through, 0.0), first[d])


def inside_kernel(weight_ref, r_ref, got_ref, f_ref, xs_ref, base_ref, cm_ref, b_ref, c_ref):
    weight = rate_lanes(weight_ref)
    key_rows, key_cols, first, _ = keys_of(r_ref)
    for q in range(PEERS):
        src = (q % 2) * 4 + q // 2
        sl = slice(q * TOK, (q + 1) * TOK)
        b_ref[sl, :] = r_ref[src, :TOK, WIDE : 2 * WIDE]
        c = got_ref[src]
        c_ref[sl, :] = c
        for d in range(2):
            fm = ones_where(key_cols[q] == first[d] + 4.0 * d, BF16)
            for half in range(2):
                at = d * WIDE + half * TOK
                cm_ref[sl, at : at + TOK] = c[:, half * TOK : (half + 1) * TOK] * fm
    causal = iota((256, 256), 0) >= iota((256, 256), 1)
    for i in range(4):
        si = slice(i * 256, (i + 1) * 256)
        acc = jnp.zeros((256, WIDE), F32)
        keys = jnp.concatenate([jnp.concatenate([key_cols[2 * i + n]] * 2, axis=1) for n in range(2)], axis=0)
        for j in range(i + 1):
            sj = slice(j * 256, (j + 1) * 256)
            s = dot(c_ref[si, :], b_ref[sj, :], ((1,), (1,)))
            same = keys == jnp.concatenate(key_rows[2 * j : 2 * j + 2], axis=1)
            w = jnp.where(same & causal if i == j else same, s, 0.0).astype(BF16)
            acc = acc + dot(w, xs_ref[sj, :], ((1,), (0,)))
        acc = acc * f_ref[si, :]
        for s in range(2):
            x = r_ref[s * 4 + i, :TOK, 0:WIDE].astype(F32)
            at = i * 256 + s * TOK
            base_ref[at : at + TOK, :] = acc[s * TOK : (s + 1) * TOK] + weight * x


def pass_kernel(e_ref, own_ref, out_ref):
    for d in range(2):
        joined = e_ref[d, WIDE : WIDE + 1, :].astype(F32) == own_ref[d, 1:2, :]
        through = jnp.where(joined, own_ref[d, 0:1, :], 0.0)
        out_ref[d] = (through * e_ref[d, 0:WIDE, :].astype(F32)).astype(BF16)


def carry_kernel(base_ref, f_ref, cm_ref, e1_ref, e2_ref, own_ref, y_ref, h_ref):
    for d in range(2):
        joined = e1_ref[d, WIDE : WIDE + 1, :].astype(F32) == own_ref[d, 1:2, :]
        h = e1_ref[d, 0:WIDE, :].astype(F32) + e2_ref[d].astype(F32)
        h_ref[d * WIDE : (d + 1) * WIDE, :] = jnp.where(joined, h, 0.0).astype(BF16)
    for q in range(PEERS):
        sl = slice(q * TOK, (q + 1) * TOK)
        y = base_ref[sl, :] + f_ref[sl, :] * dot(cm_ref[sl, :], h_ref[...], ((1,), (0,)))
        y_ref[(q % 2) * 4 + q // 2] = y.astype(BF16)


def square_kernel(y_ref, s_ref):
    acc = jnp.zeros((TOK, WIDE), F32)
    for o in range(PEERS):
        v = y_ref[o].astype(F32)
        acc = acc + v * v
    s_ref[...] = dot(jnp.ones((AUX, WIDE), F32), acc, ((1,), (1,)), HIGH)


def add_kernel(a_ref, b_ref, out_ref):
    out_ref[...] = a_ref[...] + b_ref[...]


def scale_kernel(y_ref, s0_ref, s1_ref, gain_ref, out_ref, *, features):
    total = s0_ref[...] + s1_ref[...]
    pick = ones_where(iota((AUX, TOK), 0) == 0)
    col = dot(total, pick, ((0,), (0,)), HIGH)
    scale = lax.rsqrt(col / features + EPSILON)
    scale = jnp.concatenate([scale, scale], axis=1)
    for o in range(PEERS):
        sl = slice(o * WIDE, (o + 1) * WIDE)
        out_ref[:, sl] = (y_ref[o].astype(F32) * scale * gain_ref[:, sl]).astype(BF16)


VM = pl.BlockSpec(memory_space=pltpu.VMEM)
SM = pl.BlockSpec(memory_space=pltpu.SMEM)
HB = pl.BlockSpec(memory_space=pl.ANY)


def kept(x):
    return pltpu.with_memory_space_constraint(x, pltpu.VMEM)


def far(x):
    return pltpu.with_memory_space_constraint(x, pltpu.HBM)


def call(kernel, specs, outs, *args, scratch=()):
    return pl.pallas_call(
        kernel,
        in_specs=specs,
        out_specs=[VM] * len(outs),
        out_shape=outs,
        scratch_shapes=list(scratch),
        compiler_params=pltpu.CompilerParams(vmem_limit_bytes=14 << 20),
    )(*args)


def whole(tokens, bc_proj, step_sizes, decay_rates, direct_weight, norm_gain, routes, segments):
    V = pltpu.VMEM
    pairs = bc_proj.reshape(TOK, 2, 4, TOK).transpose(0, 2, 1, 3).reshape(8 * TOK, TOK)
    send, send_c = call(
        pack_kernel,
        [HB] * 5,
        [V((PEERS, TOK + AUX, 2 * WIDE), BF16), pltpu.HBM((PEERS, TOK, WIDE), BF16)],
        far(tokens[0]), far(pairs), far(step_sizes[0]), far(routes.reshape(1, 16)), far(segments),
        scratch=[
            V((8 * TOK, TOK), BF16),
            V((16, 256), BF16),
            V((1, 16), jnp.int32),
            V((1, 256), jnp.int32),
            V((8 * TOK, TOK), F32),
            pltpu.SemaphoreType.DMA((4 + PEERS,)),
        ],
    )
    got = kept(lax.all_to_all(send, ("dp", "y"), split_axis=0, concat_axis=0, tiled=True))
    e, f, xs, own = call(
        state_kernel,
        [SM, VM],
        [pltpu.HBM((2, WIDE + AUX, WIDE), BF16), V((SPAN, WIDE), F32), V((SPAN, WIDE), BF16), V((2, AUX, WIDE), F32)],
        decay_rates, got,
        scratch=[V((2, WIDE, SPAN), BF16)],
    )
    f, xs, own = kept(f), kept(xs), kept(own)
    e, send_c = lax.optimization_barrier((e, send_c))
    e1 = kept(lax.ppermute(e, "z", [(i, i + 1) for i in range(3)]))
    got_c = far(lax.all_to_all(send_c, ("dp", "y"), split_axis=0, concat_axis=0, tiled=True))
    (older,) = call(pass_kernel, [VM, VM], [pltpu.HBM((2, WIDE, WIDE), BF16)], e1, own)
    e2 = kept(lax.ppermute(older, "z", [(i, i + 1) for i in range(1, 3)]))
    base, cm = call(
        inside_kernel,
        [SM] + [VM] * 4,
        [V((SPAN, WIDE), F32), V((SPAN, 2 * WIDE), BF16)],
        direct_weight, got, got_c, f, xs,
        scratch=[V((SPAN, WIDE), BF16), V((SPAN, WIDE), BF16)],
    )
    (out,) = call(
        carry_kernel,
        [VM] * 6,
        [V((PEERS, TOK, WIDE), BF16)],
        kept(base), f, kept(cm), e1, e2, own,
        scratch=[V((2 * WIDE, WIDE), BF16)],
    )
    back = kept(lax.all_to_all(out, ("dp", "y"), split_axis=0, concat_axis=0, tiled=True))
    (s0,) = call(square_kernel, [VM], [V((AUX, TOK), F32)], back)
    t0 = lax.ppermute(s0, "tensor", [(i, i ^ 1) for i in range(4)])
    (s0,) = call(add_kernel, [VM] * 2, [V((AUX, TOK), F32)], kept(s0), kept(t0))
    others = [kept(lax.ppermute(s0, "tensor", [(i, i ^ 2) for i in range(4)]))]

    def scale(*refs):
        scale_kernel(*refs, features=128 * 64)

    out_shape = [jax.ShapeDtypeStruct((TOK, PEERS * WIDE), BF16)]
    (mixed,) = call(scale, [VM] * 4, out_shape, back, kept(s0), *others, norm_gain[None])
    return mixed[None]


def solution(mesh):
    fine = Mesh(mesh.devices.reshape(2, 4, 4, 4), ("dp", "z", "y", "tensor"))
    rows = ("z", "y")
    return jax.shard_map(
        whole,
        mesh=fine,
        in_specs=(
            P("dp", rows, "tensor"),
            P("dp", rows, None, "tensor"),
            P("dp", rows, "tensor"),
            P("tensor"),
            P("tensor"),
            P("tensor"),
            P("dp", rows, None),
            P("dp", rows),
        ),
        out_specs=P("dp", rows, "tensor"),
        check_vma=False,
    )
```

```python
import jax
import jax.numpy as jnp
from jax import lax
from jax.experimental import pallas as pl
from jax.experimental.pallas import tpu as pltpu
from jax.sharding import Mesh, PartitionSpec as P


EPSILON = 1e-05
F32 = jnp.float32
BF16 = jnp.bfloat16
HIGH = lax.Precision.HIGHEST
TOK = 128
PEERS = 8
SPAN = TOK * PEERS
WIDE = 256
AUX = 8


def dot(a, b, dims, precision=None):
    return lax.dot_general(a, b, (dims, ((), ())), precision=precision, preferred_element_type=F32)


def iota(shape, dim):
    return lax.broadcasted_iota(jnp.int32, shape, dim)


def ones_where(cond, dtype=F32):
    return jnp.where(cond, 1.0, 0.0).astype(dtype)


def pack_kernel(
    tok_ref, bc_ref, dt_ref, route_ref, seg_ref, out_ref, c_ref, bc_buf, dt_buf, route_buf, seg_buf, wide_ref, c_buf, sems
):
    small = ((bc_ref, bc_buf), (route_ref, route_buf), (dt_ref, dt_buf), (seg_ref, seg_buf))
    copies = [pltpu.make_async_copy(a, b, sems.at[n]) for n, (a, b) in enumerate(small)]
    for o in range(PEERS):
        src = tok_ref.at[:, o * WIDE : (o + 1) * WIDE]
        copies.append(pltpu.make_async_copy(src, out_ref.at[o, 0:TOK, 0:WIDE], sems.at[4 + o]))
    for copy in copies:
        copy.start()
    copies[0].wait()
    wide_ref[...] = bc_buf[...].astype(F32)
    for tile in range(4):
        g, half = tile // 2, tile % 2
        c_buf[g, :, half * TOK : (half + 1) * TOK] = wide_ref[pl.ds(2 * tile + 1, TOK, stride=8), :].astype(BF16)
    for o in range(PEERS):
        copies.append(pltpu.make_async_copy(c_buf.at[o // 4], c_ref.at[o], sems.at[4 + PEERS + o]))
        copies[-1].start()
    for tile in range(4):
        g, half = tile // 2, tile % 2
        b = wide_ref[pl.ds(2 * tile, TOK, stride=8), :].astype(BF16)
        for o in range(g * 4, g * 4 + 4):
            out_ref[o, :TOK, WIDE + half * TOK : WIDE + (half + 1) * TOK] = b
    for copy in copies[1:4]:
        copy.wait()
    block_of = ones_where(iota((16, TOK), 1) // 8 == iota((16, TOK), 0), BF16)
    spread = dot(dt_buf[...], block_of, ((0,), (0,)))
    same_u = iota((256, TOK), 0) % 8 == iota((256, TOK), 1) % 8
    spread = jnp.where(same_u, spread, 0.0).astype(BF16)
    head_of = ones_where(iota((32, 256), 1) // 8 == iota((32, 256), 0), BF16)
    dt_rows = dot(head_of, spread, ((1,), (0,)))
    route = jnp.broadcast_to(route_buf[...].astype(F32), (TOK, 16)).astype(BF16)
    route_row = dot(route, block_of, ((1,), (0,)))
    route_col = dot(block_of, route, ((0,), (1,)))
    ahead = (route_row == route_col) & (iota((TOK, TOK), 0) < iota((TOK, TOK), 1))
    place = jnp.sum(ones_where(ahead), axis=0, keepdims=True) + (lax.axis_index("dp") * TOK).astype(F32)
    segs = seg_buf[...]
    lane = iota((1, TOK), 1)
    starts = jnp.zeros((1, TOK), F32)
    for k in range(3):
        starts = jnp.where(lane == k, jnp.sum(ones_where(segs < k + 1), axis=1, keepdims=True), starts)
    row = iota((AUX, TOK), 0)
    for o in range(PEERS):
        aux = jnp.where(row == 4, route_row[0:1], jnp.where(row == 5, place, starts))
        for h in range(4):
            aux = jnp.where(row == h, dt_rows[o * 4 + h : o * 4 + h + 1], aux)
        out_ref[o, TOK : TOK + AUX, :] = jnp.concatenate([aux.astype(BF16)] * 4, axis=1)
    for copy in copies[4:]:
        copy.wait()


def rate_lanes(ref):
    lane = iota((1, WIDE), 1) // 64
    first = (lax.axis_index("dp") * 4 + lax.axis_index("y")) * 4
    out = jnp.full((1, WIDE), ref[first], F32)
    for h in range(1, 4):
        out = jnp.where(lane == h, ref[first + h], out)
    return out


def keys_of(r_ref):
    pick_route = ones_where(iota((AUX, TOK), 0) == 4, BF16)
    pick_place = ones_where(iota((AUX, TOK), 0) == 5, BF16)
    starts = [[None] * 3, [None] * 3]
    rows, cols = [], []
    for q in range(PEERS):
        y, j = q // 2, q % 2
        aux = r_ref[j * 4 + y, TOK : TOK + AUX, 0:TOK]
        auxf = aux.astype(F32)
        rows.append((auxf[4:5], auxf[5:6] + y * 256.0))
        cols.append((dot(aux, pick_route, ((0,), (0,))), dot(aux, pick_place, ((0,), (0,))) + y * 256.0))
        for k in range(3):
            n = auxf[6:7, k : k + 1]
            starts[j][k] = n if starts[j][k] is None else starts[j][k] + n

    def key_of(route, place):
        second = route > 0.5
        doc = 4.0 * route
        for k in range(3):
            doc = doc + ones_where(place >= jnp.where(second, starts[1][k], starts[0][k]))
        return doc

    first, last = [], []
    for d in range(2):
        first.append(sum(ones_where(starts[d][k] <= 0.0) for k in range(3)))
        last.append(sum(ones_where(starts[d][k] <= SPAN - 1.0) for k in range(3)))
    return [key_of(*p) for p in rows], [key_of(*p) for p in cols], first, last


def three(x, lane):
    top = x.astype(BF16).astype(F32)
    rest = x - top
    mid = rest.astype(BF16).astype(F32)
    return jnp.where(lane < 32, top, jnp.where(lane < 64, mid, jnp.where(lane < 96, rest - mid, 0.0))).astype(BF16)


def state_kernel(rate_ref, r_ref, e_ref, f_ref, xs_ref, own_ref, bt_ref):
    rate = rate_lanes(rate_ref)
    lane = iota((1, TOK), 1)
    key = lane % 32 // 4
    row, col = iota((AUX, TOK), 0), iota((AUX, TOK), 1)
    code_of = jnp.where(row == 5, 1.0, jnp.where(row == 4, 2048.0, 0.0)).astype(BF16)
    dt_of = ones_where(row == col % 4, BF16)
    spread = ones_where(iota((AUX, WIDE), 1) // 64 == iota((AUX, WIDE), 0), BF16)
    columns = jnp.concatenate([code_of, dt_of, spread], axis=1)
    expand = ones_where(iota((TOK, WIDE), 0) % 4 == iota((TOK, WIDE), 1) // 64, BF16)
    lower = ones_where(iota((256, 256), 0) >= iota((256, 256), 1), BF16)
    auxs = [r_ref[q % 2 * 4 + q // 2, TOK : TOK + AUX, 0:TOK] for q in range(PEERS)]
    auxf = [a.astype(F32) for a in auxs]
    starts = [[sum(auxf[2 * y + d][6:7, k : k + 1] for y in range(4)) for k in range(3)] for d in range(2)]
    first = [sum(ones_where(starts[d][k] <= 0.0) for k in range(3)) for d in range(2)]
    last = [sum(ones_where(starts[d][k] <= SPAN - 1.0) for k in range(3)) for d in range(2)]
    low, high = jnp.zeros((1, TOK), F32), jnp.zeros((1, TOK), F32)
    final = []
    for d in range(2):
        edges = [jnp.zeros((1, 1), F32)] + starts[d] + [jnp.full((1, 1), float(SPAN), F32)]
        at = edges[0]
        for n in range(4):
            low = jnp.where(key == 4 * d + n, edges[n] + 2048.0 * d, low)
            high = jnp.where(key == 4 * d + n, edges[n + 1] + 2048.0 * d, high)
            at = jnp.where(last[d] == n, edges[n], at)
        final.append(at + 2048.0 * d)
    for q in range(PEERS):
        code = auxf[q][4:5] * 2048.0 + auxf[q][5:6] + (q // 2) * 256.0
        bt = jnp.transpose(r_ref[q % 2 * 4 + q // 2, :TOK, WIDE : 2 * WIDE])
        for d in range(2):
            ends = jnp.broadcast_to(ones_where((code >= final[d]) & (code < 2048.0 * (d + 1))), (16, TOK)).astype(BF16)
            bt_ref[d, :, q * TOK : (q + 1) * TOK] = bt * ends[0:1]
    total = jnp.zeros((1, TOK), F32)
    for b in range(4):
        parts = [dot(auxs[2 * b + s], columns, ((0,), (0,))) for s in range(2)]
        part = jnp.concatenate(parts, axis=0)
        code = part[:, 0:TOK] + b * 256.0
        mine = (code >= low) & (code < high)
        z = jnp.where(mine, part[:, TOK : 2 * TOK], 0.0).astype(BF16)
        sums = dot(lower, z, ((1,), (0,))) + total
        total = sums[255:256]
        d_wide = dot(three(jnp.where(mine, sums, 0.0), lane), expand, ((1,), (0,)))
        f_ref[b * 256 : (b + 1) * 256, :] = jnp.exp(-rate * d_wide).astype(BF16)
        grow = jnp.exp(rate * d_wide) * part[:, 2 * TOK :]
        for s in range(2):
            x = r_ref[s * 4 + b, :TOK, 0:WIDE].astype(F32)
            at = b * 256 + s * TOK
            xs_ref[at : at + TOK, :] = (x * grow[s * TOK : (s + 1) * TOK]).astype(BF16)
    row8 = iota((AUX, WIDE), 0)
    for d in range(2):
        tail = jnp.broadcast_to(jnp.where(key == last[d].astype(jnp.int32) + 4 * d, total, 0.0), (AUX, TOK))
        through = jnp.exp(-rate * dot(three(tail, lane), expand, ((1,), (0,))))
        e = dot(bt_ref[d], xs_ref[...], ((1,), (0,))) * through[0:1]
        e_ref[d, 0:WIDE, :] = e.astype(BF16)
        e_ref[d, WIDE : WIDE + AUX, :] = jnp.broadcast_to(last[d], (AUX, WIDE)).astype(BF16)
        own_ref[d] = jnp.where(row8 == 0, jnp.where(first[d] == last[d], through, 0.0), first[d])


def inside_kernel(weight_ref, r_ref, got_ref, f_ref, xs_ref, base_ref, cm_ref, b_ref, c_ref):
    weight = rate_lanes(weight_ref)
    key_rows, key_cols, first, _ = keys_of(r_ref)
    for q in range(PEERS):
        src = (q % 2) * 4 + q // 2
        sl = slice(q * TOK, (q + 1) * TOK)
        b_ref[sl, :] = r_ref[src, :TOK, WIDE : 2 * WIDE]
        c = got_ref[src]
        c_ref[sl, :] = c
        for d in range(2):
            fm = ones_where(key_cols[q] == first[d] + 4.0 * d, BF16)
            for half in range(2):
                at = d * WIDE + half * TOK
                cm_ref[sl, at : at + TOK] = c[:, half * TOK : (half + 1) * TOK] * fm
    causal = iota((256, 256), 0) >= iota((256, 256), 1)
    for i in range(4):
        si = slice(i * 256, (i + 1) * 256)
        acc = jnp.zeros((256, WIDE), F32)
        keys = jnp.concatenate([jnp.concatenate([key_cols[2 * i + n]] * 2, axis=1) for n in range(2)], axis=0)
        for j in range(i + 1):
            sj = slice(j * 256, (j + 1) * 256)
            s = dot(c_ref[si, :], b_ref[sj, :], ((1,), (1,)))
            same = keys == jnp.concatenate(key_rows[2 * j : 2 * j + 2], axis=1)
            w = jnp.where(same & causal if i == j else same, s, 0.0).astype(BF16)
            acc = acc + dot(w, xs_ref[sj, :], ((1,), (0,)))
        acc = acc * f_ref[si, :].astype(F32)
        for s in range(2):
            x = r_ref[s * 4 + i, :TOK, 0:WIDE].astype(F32)
            at = i * 256 + s * TOK
            base_ref[at : at + TOK, :] = acc[s * TOK : (s + 1) * TOK] + weight * x


def pass_kernel(e_ref, own_ref, out_ref):
    for d in range(2):
        joined = e_ref[d, WIDE : WIDE + 1, :].astype(F32) == own_ref[d, 1:2, :]
        through = jnp.where(joined, own_ref[d, 0:1, :], 0.0)
        out_ref[d] = (through * e_ref[d, 0:WIDE, :].astype(F32)).astype(BF16)


def carry_kernel(base_ref, f_ref, cm_ref, e1_ref, e2_ref, own_ref, y_ref, h_ref):
    for d in range(2):
        joined = e1_ref[d, WIDE : WIDE + 1, :].astype(F32) == own_ref[d, 1:2, :]
        h = e1_ref[d, 0:WIDE, :].astype(F32) + e2_ref[d].astype(F32)
        h_ref[d * WIDE : (d + 1) * WIDE, :] = jnp.where(joined, h, 0.0).astype(BF16)
    for q in range(PEERS):
        sl = slice(q * TOK, (q + 1) * TOK)
        y = base_ref[sl, :] + f_ref[sl, :].astype(F32) * dot(cm_ref[sl, :], h_ref[...], ((1,), (0,)))
        y_ref[(q % 2) * 4 + q // 2] = y.astype(BF16)


def square_kernel(y_ref, s_ref):
    acc = jnp.zeros((TOK, WIDE), F32)
    for o in range(PEERS):
        v = y_ref[o].astype(F32)
        acc = acc + v * v
    s_ref[...] = dot(jnp.ones((AUX, WIDE), F32), acc, ((1,), (1,)), HIGH)


def add_kernel(a_ref, b_ref, out_ref):
    out_ref[...] = a_ref[...] + b_ref[...]


def scale_kernel(y_ref, s0_ref, s1_ref, gain_ref, out_ref, *, features):
    total = s0_ref[...] + s1_ref[...]
    pick = ones_where(iota((AUX, TOK), 0) == 0)
    col = dot(total, pick, ((0,), (0,)), HIGH)
    scale = lax.rsqrt(col / features + EPSILON)
    scale = jnp.concatenate([scale, scale], axis=1)
    for o in range(PEERS):
        sl = slice(o * WIDE, (o + 1) * WIDE)
        out_ref[:, sl] = (y_ref[o].astype(F32) * scale * gain_ref[:, sl]).astype(BF16)


VM = pl.BlockSpec(memory_space=pltpu.VMEM)
SM = pl.BlockSpec(memory_space=pltpu.SMEM)
HB = pl.BlockSpec(memory_space=pl.ANY)


def kept(x):
    return pltpu.with_memory_space_constraint(x, pltpu.VMEM)


def far(x):
    return pltpu.with_memory_space_constraint(x, pltpu.HBM)


def call(kernel, specs, outs, *args, scratch=(), out_specs=None):
    return pl.pallas_call(
        kernel,
        in_specs=specs,
        out_specs=out_specs or [VM] * len(outs),
        out_shape=outs,
        scratch_shapes=list(scratch),
        compiler_params=pltpu.CompilerParams(vmem_limit_bytes=14 << 20),
    )(*args)


def whole(tokens, bc_proj, step_sizes, decay_rates, direct_weight, norm_gain, routes, segments):
    V = pltpu.VMEM
    pairs = bc_proj.reshape(TOK, 2, 4, TOK).transpose(0, 2, 1, 3).reshape(8 * TOK, TOK)
    send, send_c = call(
        pack_kernel,
        [HB] * 5,
        [V((PEERS, TOK + AUX, 2 * WIDE), BF16), pltpu.HBM((PEERS, TOK, WIDE), BF16)],
        far(tokens[0]), far(pairs), far(step_sizes[0]), far(routes.reshape(1, 16)), far(segments),
        scratch=[
            V((8 * TOK, TOK), BF16),
            V((16, 256), BF16),
            V((1, 16), jnp.int32),
            V((1, 256), jnp.int32),
            V((8 * TOK, TOK), F32),
            V((2, TOK, WIDE), BF16),
            pltpu.SemaphoreType.DMA((4 + 2 * PEERS,)),
        ],
        out_specs=[VM, HB],
    )
    got = kept(lax.all_to_all(send, ("dp", "y"), split_axis=0, concat_axis=0, tiled=True))
    e, f, xs, own = call(
        state_kernel,
        [SM, VM],
        [V((2, WIDE + AUX, WIDE), BF16), V((SPAN, WIDE), BF16), V((SPAN, WIDE), BF16), V((2, AUX, WIDE), F32)],
        decay_rates, got,
        scratch=[V((2, WIDE, SPAN), BF16)],
    )
    f, xs, own = kept(f), kept(xs), kept(own)
    e, send_c = lax.optimization_barrier((e, send_c))
    e1 = kept(lax.ppermute(e, "z", [(i, i + 1) for i in range(3)]))
    got_c = kept(lax.all_to_all(send_c, ("dp", "y"), split_axis=0, concat_axis=0, tiled=True))
    (older,) = call(pass_kernel, [VM, VM], [V((2, WIDE, WIDE), BF16)], e1, own)
    e2 = kept(lax.ppermute(older, "z", [(i, i + 1) for i in range(1, 3)]))
    base, cm = call(
        inside_kernel,
        [SM] + [VM] * 4,
        [V((SPAN, WIDE), F32), V((SPAN, 2 * WIDE), BF16)],
        direct_weight, got, got_c, f, xs,
        scratch=[V((SPAN, WIDE), BF16), V((SPAN, WIDE), BF16)],
    )
    (out,) = call(
        carry_kernel,
        [VM] * 6,
        [V((PEERS, TOK, WIDE), BF16)],
        kept(base), f, kept(cm), e1, e2, own,
        scratch=[V((2 * WIDE, WIDE), BF16)],
    )
    back = kept(lax.all_to_all(out, ("dp", "y"), split_axis=0, concat_axis=0, tiled=True))
    (s0,) = call(square_kernel, [VM], [V((AUX, TOK), F32)], back)
    t0 = lax.ppermute(s0, "tensor", [(i, i ^ 1) for i in range(4)])
    (s0,) = call(add_kernel, [VM] * 2, [V((AUX, TOK), F32)], kept(s0), kept(t0))
    others = [kept(lax.ppermute(s0, "tensor", [(i, i ^ 2) for i in range(4)]))]

    def scale(*refs):
        scale_kernel(*refs, features=128 * 64)

    out_shape = [jax.ShapeDtypeStruct((TOK, PEERS * WIDE), BF16)]
    (mixed,) = call(scale, [VM] * 4, out_shape, back, kept(s0), *others, norm_gain[None])
    return mixed[None]


def solution(mesh):
    fine = Mesh(mesh.devices.reshape(2, 4, 4, 4), ("dp", "z", "y", "tensor"))
    rows = ("z", "y")
    return jax.shard_map(
        whole,
        mesh=fine,
        in_specs=(
            P("dp", rows, "tensor"),
            P("dp", rows, None, "tensor"),
            P("dp", rows, "tensor"),
            P("tensor"),
            P("tensor"),
            P("tensor"),
            P("dp", rows, None),
            P("dp", rows),
        ),
        out_specs=P("dp", rows, "tensor"),
        check_vma=False,
    )
```

```python
import jax
import jax.numpy as jnp
from jax import lax
from jax.experimental import pallas as pl
from jax.experimental.pallas import tpu as pltpu
from jax.sharding import Mesh, PartitionSpec as P


EPSILON = 1e-05
F32 = jnp.float32
BF16 = jnp.bfloat16
HIGH = lax.Precision.HIGHEST
TOK = 128
PEERS = 8
SPAN = TOK * PEERS
WIDE = 256
AT = 2 * TOK
AUX = 8


def dot(a, b, dims, precision=None):
    return lax.dot_general(a, b, (dims, ((), ())), precision=precision, preferred_element_type=F32)


def iota(shape, dim):
    return lax.broadcasted_iota(jnp.int32, shape, dim)


def ones_where(cond, dtype=F32):
    return jnp.where(cond, 1.0, 0.0).astype(dtype)


def pack_kernel(
    tok_ref, bc_ref, dt_ref, route_ref, seg_ref, out_ref, c_ref, bc_buf, dt_buf, route_buf, seg_buf, wide_ref, c_buf, sems
):
    small = ((bc_ref, bc_buf), (route_ref, route_buf), (dt_ref, dt_buf), (seg_ref, seg_buf))
    copies = [pltpu.make_async_copy(a, b, sems.at[n]) for n, (a, b) in enumerate(small)]
    for o in range(PEERS):
        src = tok_ref.at[:, o * WIDE : (o + 1) * WIDE]
        copies.append(pltpu.make_async_copy(src, out_ref.at[o, 0:TOK, 0:WIDE], sems.at[4 + o]))
    for copy in copies:
        copy.start()
    copies[0].wait()
    wide_ref[...] = bc_buf[...].astype(F32)
    for tile in range(4):
        g, half = tile // 2, tile % 2
        c_buf[g, :, half * TOK : (half + 1) * TOK] = wide_ref[pl.ds(2 * tile + 1, TOK, stride=8), :].astype(BF16)
    for o in range(PEERS):
        copies.append(pltpu.make_async_copy(c_buf.at[o // 4], c_ref.at[o], sems.at[4 + PEERS + o]))
        copies[-1].start()
    for tile in range(4):
        g, half = tile // 2, tile % 2
        b = wide_ref[pl.ds(2 * tile, TOK, stride=8), :].astype(BF16)
        for o in range(g * 4, g * 4 + 4):
            out_ref[o, TOK:AT, half * TOK : (half + 1) * TOK] = b
    for copy in copies[1:4]:
        copy.wait()
    block_of = ones_where(iota((16, TOK), 1) // 8 == iota((16, TOK), 0), BF16)
    spread = dot(dt_buf[...], block_of, ((0,), (0,)))
    same_u = iota((256, TOK), 0) % 8 == iota((256, TOK), 1) % 8
    spread = jnp.where(same_u, spread, 0.0).astype(BF16)
    head_of = ones_where(iota((32, 256), 1) // 8 == iota((32, 256), 0), BF16)
    dt_rows = dot(head_of, spread, ((1,), (0,)))
    route = jnp.broadcast_to(route_buf[...].astype(F32), (TOK, 16)).astype(BF16)
    route_row = dot(route, block_of, ((1,), (0,)))
    route_col = dot(block_of, route, ((0,), (1,)))
    ahead = (route_row == route_col) & (iota((TOK, TOK), 0) < iota((TOK, TOK), 1))
    place = jnp.sum(ones_where(ahead), axis=0, keepdims=True) + (lax.axis_index("dp") * TOK).astype(F32)
    segs = seg_buf[...]
    lane = iota((1, TOK), 1)
    starts = jnp.zeros((1, TOK), F32)
    for k in range(3):
        starts = jnp.where(lane == k, jnp.sum(ones_where(segs < k + 1), axis=1, keepdims=True), starts)
    row = iota((AUX, TOK), 0)
    for o in range(PEERS):
        aux = jnp.where(row == 4, route_row[0:1], jnp.where(row == 5, place, starts))
        for h in range(4):
            aux = jnp.where(row == h, dt_rows[o * 4 + h : o * 4 + h + 1], aux)
        out_ref[o, AT : AT + AUX, :] = jnp.concatenate([aux.astype(BF16)] * 2, axis=1)
    for copy in copies[4:]:
        copy.wait()


def rate_lanes(ref):
    lane = iota((1, WIDE), 1) // 64
    first = (lax.axis_index("dp") * 4 + lax.axis_index("y")) * 4
    out = jnp.full((1, WIDE), ref[first], F32)
    for h in range(1, 4):
        out = jnp.where(lane == h, ref[first + h], out)
    return out


def keys_of(r_ref):
    auxf = [r_ref[q % 2 * 4 + q // 2, AT : AT + AUX, 0:TOK].astype(F32) for q in range(PEERS)]
    starts = [[sum(auxf[2 * y + d][6:7, k : k + 1] for y in range(4)) for k in range(3)] for d in range(2)]
    first = [sum(ones_where(starts[d][k] <= 0.0) for k in range(3)) for d in range(2)]
    pick = ones_where(iota((AUX, TOK), 0) == 0, BF16)
    rows, cols = [], []
    for q in range(PEERS):
        route, place = auxf[q][4:5], auxf[q][5:6] + (q // 2) * 256.0
        doc = 4.0 * route
        for k in range(3):
            doc = doc + ones_where(place >= jnp.where(route > 0.5, starts[1][k], starts[0][k]))
        rows.append(doc)
        cols.append(dot(jnp.broadcast_to(doc, (AUX, TOK)).astype(BF16), pick, ((0,), (0,))))
    return rows, cols, first


def three(x, lane):
    top = x.astype(BF16).astype(F32)
    rest = x - top
    mid = rest.astype(BF16).astype(F32)
    return jnp.where(lane < 32, top, jnp.where(lane < 64, mid, jnp.where(lane < 96, rest - mid, 0.0))).astype(BF16)


def state_kernel(rate_ref, r_ref, e_ref, f_ref, xs_ref, own_ref, bt_ref):
    rate = rate_lanes(rate_ref)
    lane = iota((1, TOK), 1)
    key = lane % 32 // 4
    row, col = iota((AUX, TOK), 0), iota((AUX, TOK), 1)
    code_of = jnp.where(row == 5, 1.0, jnp.where(row == 4, 2048.0, 0.0)).astype(BF16)
    dt_of = ones_where(row == col % 4, BF16)
    spread = ones_where(iota((AUX, WIDE), 1) // 64 == iota((AUX, WIDE), 0), BF16)
    columns = jnp.concatenate([code_of, dt_of, spread], axis=1)
    expand = ones_where(iota((TOK, WIDE), 0) % 4 == iota((TOK, WIDE), 1) // 64, BF16)
    lower = ones_where(iota((256, 256), 0) >= iota((256, 256), 1), BF16)
    auxs = [r_ref[q % 2 * 4 + q // 2, AT : AT + AUX, 0:TOK] for q in range(PEERS)]
    auxf = [a.astype(F32) for a in auxs]
    starts = [[sum(auxf[2 * y + d][6:7, k : k + 1] for y in range(4)) for k in range(3)] for d in range(2)]
    first = [sum(ones_where(starts[d][k] <= 0.0) for k in range(3)) for d in range(2)]
    last = [sum(ones_where(starts[d][k] <= SPAN - 1.0) for k in range(3)) for d in range(2)]
    low, high = jnp.zeros((1, TOK), F32), jnp.zeros((1, TOK), F32)
    final = []
    for d in range(2):
        edges = [jnp.zeros((1, 1), F32)] + starts[d] + [jnp.full((1, 1), float(SPAN), F32)]
        at = edges[0]
        for n in range(4):
            low = jnp.where(key == 4 * d + n, edges[n] + 2048.0 * d, low)
            high = jnp.where(key == 4 * d + n, edges[n + 1] + 2048.0 * d, high)
            at = jnp.where(last[d] == n, edges[n], at)
        final.append(at + 2048.0 * d)
    for q in range(PEERS):
        code = auxf[q][4:5] * 2048.0 + auxf[q][5:6] + (q // 2) * 256.0
        bt = jnp.transpose(r_ref[q % 2 * 4 + q // 2, TOK:AT, :])
        for d in range(2):
            ends = jnp.broadcast_to(ones_where((code >= final[d]) & (code < 2048.0 * (d + 1))), (16, TOK)).astype(BF16)
            bt_ref[d, :, q * TOK : (q + 1) * TOK] = bt * ends[0:1]
    total = jnp.zeros((1, TOK), F32)
    for b in range(4):
        parts = [dot(auxs[2 * b + s], columns, ((0,), (0,))) for s in range(2)]
        part = jnp.concatenate(parts, axis=0)
        code = part[:, 0:TOK] + b * 256.0
        mine = (code >= low) & (code < high)
        z = jnp.where(mine, part[:, TOK : 2 * TOK], 0.0).astype(BF16)
        sums = dot(lower, z, ((1,), (0,))) + total
        total = sums[255:256]
        d_wide = dot(three(jnp.where(mine, sums, 0.0), lane), expand, ((1,), (0,)))
        f_ref[b * 256 : (b + 1) * 256, :] = jnp.exp(-rate * d_wide).astype(BF16)
        grow = jnp.exp(rate * d_wide) * part[:, 2 * TOK :]
        for s in range(2):
            x = r_ref[s * 4 + b, :TOK, 0:WIDE].astype(F32)
            at = b * 256 + s * TOK
            xs_ref[at : at + TOK, :] = (x * grow[s * TOK : (s + 1) * TOK]).astype(BF16)
    row8 = iota((AUX, WIDE), 0)
    for d in range(2):
        tail = jnp.broadcast_to(jnp.where(key == last[d].astype(jnp.int32) + 4 * d, total, 0.0), (AUX, TOK))
        through = jnp.exp(-rate * dot(three(tail, lane), expand, ((1,), (0,))))
        e = dot(bt_ref[d], xs_ref[...], ((1,), (0,))) * through[0:1]
        e_ref[d, 0:WIDE, :] = e.astype(BF16)
        e_ref[d, WIDE : WIDE + AUX, :] = jnp.broadcast_to(last[d], (AUX, WIDE)).astype(BF16)
        own_ref[d] = jnp.where(row8 == 0, jnp.where(first[d] == last[d], through, 0.0), first[d])


def inside_kernel(weight_ref, r_ref, got_ref, f_ref, xs_ref, base_ref, cm_ref, b_ref, c_ref):
    weight = rate_lanes(weight_ref)
    key_rows, key_cols, first = keys_of(r_ref)
    for q in range(PEERS):
        src = (q % 2) * 4 + q // 2
        sl = slice(q * TOK, (q + 1) * TOK)
        b_ref[sl, :] = r_ref[src, TOK:AT, :]
        c = got_ref[src]
        c_ref[sl, :] = c
        for d in range(2):
            fm = ones_where(key_cols[q] == first[d] + 4.0 * d, BF16)
            for half in range(2):
                at = d * WIDE + half * TOK
                cm_ref[sl, at : at + TOK] = c[:, half * TOK : (half + 1) * TOK] * fm
    causal = iota((256, 256), 0) >= iota((256, 256), 1)
    for i in range(4):
        si = slice(i * 256, (i + 1) * 256)
        acc = jnp.zeros((256, WIDE), F32)
        keys = jnp.concatenate([jnp.concatenate([key_cols[2 * i + n]] * 2, axis=1) for n in range(2)], axis=0)
        for j in range(i + 1):
            sj = slice(j * 256, (j + 1) * 256)
            s = dot(c_ref[si, :], b_ref[sj, :], ((1,), (1,)))
            same = keys == jnp.concatenate(key_rows[2 * j : 2 * j + 2], axis=1)
            w = jnp.where(same & causal if i == j else same, s, 0.0).astype(BF16)
            acc = acc + dot(w, xs_ref[sj, :], ((1,), (0,)))
        acc = acc * f_ref[si, :].astype(F32)
        for s in range(2):
            x = r_ref[s * 4 + i, :TOK, 0:WIDE].astype(F32)
            at = i * 256 + s * TOK
            base_ref[at : at + TOK, :] = acc[s * TOK : (s + 1) * TOK] + weight * x


def pass_kernel(e_ref, own_ref, out_ref):
    for d in range(2):
        joined = e_ref[d, WIDE : WIDE + 1, :].astype(F32) == own_ref[d, 1:2, :]
        through = jnp.where(joined, own_ref[d, 0:1, :], 0.0)
        out_ref[d] = (through * e_ref[d, 0:WIDE, :].astype(F32)).astype(BF16)


def carry_kernel(base_ref, f_ref, cm_ref, e1_ref, e2_ref, own_ref, y_ref, h_ref):
    for d in range(2):
        joined = e1_ref[d, WIDE : WIDE + 1, :].astype(F32) == own_ref[d, 1:2, :]
        h = e1_ref[d, 0:WIDE, :].astype(F32) + e2_ref[d].astype(F32)
        h_ref[d * WIDE : (d + 1) * WIDE, :] = jnp.where(joined, h, 0.0).astype(BF16)
    for q in range(PEERS):
        sl = slice(q * TOK, (q + 1) * TOK)
        y = base_ref[sl, :] + f_ref[sl, :].astype(F32) * dot(cm_ref[sl, :], h_ref[...], ((1,), (0,)))
        y_ref[(q % 2) * 4 + q // 2] = y.astype(BF16)


def square_kernel(y_ref, s_ref):
    acc = jnp.zeros((TOK, WIDE), F32)
    for o in range(PEERS):
        v = y_ref[o].astype(F32)
        acc = acc + v * v
    s_ref[...] = dot(jnp.ones((AUX, WIDE), F32), acc, ((1,), (1,)), HIGH)


def add_kernel(a_ref, b_ref, out_ref):
    out_ref[...] = a_ref[...] + b_ref[...]


def scale_kernel(y_ref, s0_ref, s1_ref, gain_ref, out_ref, *, features):
    total = s0_ref[...] + s1_ref[...]
    pick = ones_where(iota((AUX, TOK), 0) == 0)
    col = dot(total, pick, ((0,), (0,)), HIGH)
    scale = lax.rsqrt(col / features + EPSILON)
    scale = jnp.concatenate([scale, scale], axis=1)
    for o in range(PEERS):
        sl = slice(o * WIDE, (o + 1) * WIDE)
        out_ref[:, sl] = (y_ref[o].astype(F32) * scale * gain_ref[:, sl]).astype(BF16)


VM = pl.BlockSpec(memory_space=pltpu.VMEM)
SM = pl.BlockSpec(memory_space=pltpu.SMEM)
HB = pl.BlockSpec(memory_space=pl.ANY)


def kept(x):
    return pltpu.with_memory_space_constraint(x, pltpu.VMEM)


def far(x):
    return pltpu.with_memory_space_constraint(x, pltpu.HBM)


def call(kernel, specs, outs, *args, scratch=(), out_specs=None):
    return pl.pallas_call(
        kernel,
        in_specs=specs,
        out_specs=out_specs or [VM] * len(outs),
        out_shape=outs,
        scratch_shapes=list(scratch),
        compiler_params=pltpu.CompilerParams(vmem_limit_bytes=14 << 20),
    )(*args)


def whole(tokens, bc_proj, step_sizes, decay_rates, direct_weight, norm_gain, routes, segments):
    V = pltpu.VMEM
    pairs = bc_proj.reshape(TOK, 2, 4, TOK).transpose(0, 2, 1, 3).reshape(8 * TOK, TOK)
    send, send_c = call(
        pack_kernel,
        [HB] * 5,
        [V((PEERS, AT + AUX, WIDE), BF16), pltpu.HBM((PEERS, TOK, WIDE), BF16)],
        far(tokens[0]), far(pairs), far(step_sizes[0]), far(routes.reshape(1, 16)), far(segments),
        scratch=[
            V((8 * TOK, TOK), BF16),
            V((16, 256), BF16),
            V((1, 16), jnp.int32),
            V((1, 256), jnp.int32),
            V((8 * TOK, TOK), F32),
            V((2, TOK, WIDE), BF16),
            pltpu.SemaphoreType.DMA((4 + 2 * PEERS,)),
        ],
        out_specs=[VM, HB],
    )
    got = kept(lax.all_to_all(send, ("dp", "y"), split_axis=0, concat_axis=0, tiled=True))
    e, f, xs, own = call(
        state_kernel,
        [SM, VM],
        [V((2, WIDE + AUX, WIDE), BF16), V((SPAN, WIDE), BF16), V((SPAN, WIDE), BF16), V((2, AUX, WIDE), F32)],
        decay_rates, got,
        scratch=[V((2, WIDE, SPAN), BF16)],
    )
    f, xs, own = kept(f), kept(xs), kept(own)
    e, send_c = lax.optimization_barrier((e, send_c))
    e1 = kept(lax.ppermute(e, "z", [(i, i + 1) for i in range(3)]))
    got_c = kept(lax.all_to_all(send_c, ("dp", "y"), split_axis=0, concat_axis=0, tiled=True))
    (older,) = call(pass_kernel, [VM, VM], [V((2, WIDE, WIDE), BF16)], e1, own)
    e2 = kept(lax.ppermute(older, "z", [(i, i + 1) for i in range(1, 3)]))
    base, cm = call(
        inside_kernel,
        [SM] + [VM] * 4,
        [V((SPAN, WIDE), F32), V((SPAN, 2 * WIDE), BF16)],
        direct_weight, got, got_c, f, xs,
        scratch=[V((SPAN, WIDE), BF16), V((SPAN, WIDE), BF16)],
    )
    (out,) = call(
        carry_kernel,
        [VM] * 6,
        [V((PEERS, TOK, WIDE), BF16)],
        kept(base), f, kept(cm), e1, e2, own,
        scratch=[V((2 * WIDE, WIDE), BF16)],
    )
    back = kept(lax.all_to_all(out, ("dp", "y"), split_axis=0, concat_axis=0, tiled=True))
    (s0,) = call(square_kernel, [VM], [V((AUX, TOK), F32)], back)
    t0 = lax.ppermute(s0, "tensor", [(i, i ^ 1) for i in range(4)])
    (s0,) = call(add_kernel, [VM] * 2, [V((AUX, TOK), F32)], kept(s0), kept(t0))
    others = [kept(lax.ppermute(s0, "tensor", [(i, i ^ 2) for i in range(4)]))]

    def scale(*refs):
        scale_kernel(*refs, features=128 * 64)

    out_shape = [jax.ShapeDtypeStruct((TOK, PEERS * WIDE), BF16)]
    (mixed,) = call(scale, [VM] * 4, out_shape, back, kept(s0), *others, norm_gain[None])
    return mixed[None]


def solution(mesh):
    fine = Mesh(mesh.devices.reshape(2, 4, 4, 4), ("dp", "z", "y", "tensor"))
    rows = ("z", "y")
    return jax.shard_map(
        whole,
        mesh=fine,
        in_specs=(
            P("dp", rows, "tensor"),
            P("dp", rows, None, "tensor"),
            P("dp", rows, "tensor"),
            P("tensor"),
            P("tensor"),
            P("tensor"),
            P("dp", rows, None),
            P("dp", rows),
        ),
        out_specs=P("dp", rows, "tensor"),
        check_vma=False,
    )
```

```python
import jax
import jax.numpy as jnp
from jax import lax
from jax.experimental import pallas as pl
from jax.experimental.pallas import tpu as pltpu
from jax.sharding import Mesh, PartitionSpec as P


EPSILON = 1e-05
F32 = jnp.float32
BF16 = jnp.bfloat16
HIGH = lax.Precision.HIGHEST
TOK = 128
PEERS = 8
SPAN = TOK * PEERS
WIDE = 256
AT = 2 * TOK
AUX = 8


def dot(a, b, dims, precision=None):
    return lax.dot_general(a, b, (dims, ((), ())), precision=precision, preferred_element_type=F32)


def iota(shape, dim):
    return lax.broadcasted_iota(jnp.int32, shape, dim)


def ones_where(cond, dtype=F32):
    return jnp.where(cond, 1.0, 0.0).astype(dtype)


def pack_kernel(
    tok_ref, bc_ref, dt_ref, route_ref, seg_ref, out_ref, c_ref, bc_buf, dt_buf, route_buf, seg_buf, wide_ref, c_buf, sems
):
    small = ((bc_ref, bc_buf), (route_ref, route_buf), (dt_ref, dt_buf), (seg_ref, seg_buf))
    copies = [pltpu.make_async_copy(a, b, sems.at[n]) for n, (a, b) in enumerate(small)]
    for o in range(PEERS):
        src = tok_ref.at[:, o * WIDE : (o + 1) * WIDE]
        copies.append(pltpu.make_async_copy(src, out_ref.at[o, 0:TOK, 0:WIDE], sems.at[4 + o]))
    for copy in copies:
        copy.start()
    copies[0].wait()
    wide_ref[...] = bc_buf[...].astype(F32)
    for tile in range(4):
        g, half = tile // 2, tile % 2
        c_buf[g, :, half * TOK : (half + 1) * TOK] = wide_ref[pl.ds(2 * tile + 1, TOK, stride=8), :].astype(BF16)
    for o in range(PEERS):
        copies.append(pltpu.make_async_copy(c_buf.at[o // 4], c_ref.at[o], sems.at[4 + PEERS + o]))
        copies[-1].start()
    for tile in range(4):
        g, half = tile // 2, tile % 2
        b = wide_ref[pl.ds(2 * tile, TOK, stride=8), :].astype(BF16)
        for o in range(g * 4, g * 4 + 4):
            out_ref[o, TOK:AT, half * TOK : (half + 1) * TOK] = b
    for copy in copies[1:4]:
        copy.wait()
    block_of = ones_where(iota((16, TOK), 1) // 8 == iota((16, TOK), 0), BF16)
    spread = dot(dt_buf[...], block_of, ((0,), (0,)))
    same_u = iota((256, TOK), 0) % 8 == iota((256, TOK), 1) % 8
    spread = jnp.where(same_u, spread, 0.0).astype(BF16)
    head_of = ones_where(iota((32, 256), 1) // 8 == iota((32, 256), 0), BF16)
    dt_rows = dot(head_of, spread, ((1,), (0,)))
    route = jnp.broadcast_to(route_buf[...].astype(F32), (TOK, 16)).astype(BF16)
    route_row = dot(route, block_of, ((1,), (0,)))
    route_col = dot(block_of, route, ((0,), (1,)))
    ahead = (route_row == route_col) & (iota((TOK, TOK), 0) < iota((TOK, TOK), 1))
    place = jnp.sum(ones_where(ahead), axis=0, keepdims=True) + (lax.axis_index("dp") * TOK).astype(F32)
    segs = seg_buf[...]
    lane = iota((1, TOK), 1)
    starts = jnp.zeros((1, TOK), F32)
    for k in range(3):
        starts = jnp.where(lane == k, jnp.sum(ones_where(segs < k + 1), axis=1, keepdims=True), starts)
    row = iota((AUX, TOK), 0)
    for o in range(PEERS):
        aux = jnp.where(row == 4, route_row[0:1], jnp.where(row == 5, place, starts))
        for h in range(4):
            aux = jnp.where(row == h, dt_rows[o * 4 + h : o * 4 + h + 1], aux)
        out_ref[o, AT : AT + AUX, :] = jnp.concatenate([aux.astype(BF16)] * 2, axis=1)
    for copy in copies[4:]:
        copy.wait()


def rate_lanes(ref):
    lane = iota((1, WIDE), 1) // 64
    first = (lax.axis_index("dp") * 4 + lax.axis_index("y")) * 4
    out = jnp.full((1, WIDE), ref[first], F32)
    for h in range(1, 4):
        out = jnp.where(lane == h, ref[first + h], out)
    return out


def keys_of(r_ref):
    auxf = [r_ref[q % 2 * 4 + q // 2, AT : AT + AUX, 0:TOK].astype(F32) for q in range(PEERS)]
    starts = [[sum(auxf[2 * y + d][6:7, k : k + 1] for y in range(4)) for k in range(3)] for d in range(2)]
    first = [sum(ones_where(starts[d][k] <= 0.0) for k in range(3)) for d in range(2)]
    pick = ones_where(iota((AUX, TOK), 0) == 0, BF16)
    rows, cols = [], []
    for q in range(PEERS):
        route, place = auxf[q][4:5], auxf[q][5:6] + (q // 2) * 256.0
        doc = 4.0 * route
        for k in range(3):
            doc = doc + ones_where(place >= jnp.where(route > 0.5, starts[1][k], starts[0][k]))
        rows.append(doc)
        cols.append(dot(jnp.broadcast_to(doc, (AUX, TOK)).astype(BF16), pick, ((0,), (0,))))
    return rows, cols, first


def three(x, lane):
    top = x.astype(BF16).astype(F32)
    rest = x - top
    mid = rest.astype(BF16).astype(F32)
    return jnp.where(lane < 32, top, jnp.where(lane < 64, mid, jnp.where(lane < 96, rest - mid, 0.0))).astype(BF16)


def state_kernel(rate_ref, r_ref, e_ref, v_ref, xs_ref, own_ref, bt_ref, v_buf, sems):
    rate = rate_lanes(rate_ref)
    lane = iota((1, TOK), 1)
    key = lane % 32 // 4
    row, col = iota((AUX, TOK), 0), iota((AUX, TOK), 1)
    code_of = jnp.where(row == 5, 1.0, jnp.where(row == 4, 2048.0, 0.0)).astype(BF16)
    dt_of = ones_where(row == col % 4, BF16)
    spread = ones_where(iota((AUX, WIDE), 1) // 64 == iota((AUX, WIDE), 0), BF16)
    columns = jnp.concatenate([code_of, dt_of, spread], axis=1)
    expand = ones_where(iota((TOK, WIDE), 0) % 4 == iota((TOK, WIDE), 1) // 64, BF16)
    lower = ones_where(iota((256, 256), 0) >= iota((256, 256), 1), BF16)
    auxs = [r_ref[q % 2 * 4 + q // 2, AT : AT + AUX, 0:TOK] for q in range(PEERS)]
    auxf = [a.astype(F32) for a in auxs]
    starts = [[sum(auxf[2 * y + d][6:7, k : k + 1] for y in range(4)) for k in range(3)] for d in range(2)]
    first = [sum(ones_where(starts[d][k] <= 0.0) for k in range(3)) for d in range(2)]
    last = [sum(ones_where(starts[d][k] <= SPAN - 1.0) for k in range(3)) for d in range(2)]
    low, high = jnp.zeros((1, TOK), F32), jnp.zeros((1, TOK), F32)
    final = []
    for d in range(2):
        edges = [jnp.zeros((1, 1), F32)] + starts[d] + [jnp.full((1, 1), float(SPAN), F32)]
        at = edges[0]
        for n in range(4):
            low = jnp.where(key == 4 * d + n, edges[n] + 2048.0 * d, low)
            high = jnp.where(key == 4 * d + n, edges[n + 1] + 2048.0 * d, high)
            at = jnp.where(last[d] == n, edges[n], at)
        final.append(at + 2048.0 * d)
    for q in range(PEERS):
        code = auxf[q][4:5] * 2048.0 + auxf[q][5:6] + (q // 2) * 256.0
        bt = jnp.transpose(r_ref[q % 2 * 4 + q // 2, TOK:AT, :])
        for d in range(2):
            ends = jnp.broadcast_to(ones_where((code >= final[d]) & (code < 2048.0 * (d + 1))), (16, TOK)).astype(BF16)
            bt_ref[d, :, q * TOK : (q + 1) * TOK] = bt * ends[0:1]
    total = jnp.zeros((1, TOK), F32)
    copies = []
    for b in range(4):
        parts = [dot(auxs[2 * b + s], columns, ((0,), (0,))) for s in range(2)]
        part = jnp.concatenate(parts, axis=0)
        code = part[:, 0:TOK] + b * 256.0
        mine = (code >= low) & (code < high)
        z = jnp.where(mine, part[:, TOK : 2 * TOK], 0.0).astype(BF16)
        sums = dot(lower, z, ((1,), (0,))) + total
        total = sums[255:256]
        v = three(jnp.where(mine, sums, 0.0), lane)
        block = slice(b * 256, (b + 1) * 256)
        v_buf[block, :] = v
        copies.append(pltpu.make_async_copy(v_buf.at[block, :], v_ref.at[block, :], sems.at[b]))
        copies[-1].start()
        d_wide = dot(v, expand, ((1,), (0,)))
        grow = jnp.exp(rate * d_wide) * part[:, 2 * TOK :]
        for s in range(2):
            x = r_ref[s * 4 + b, :TOK, 0:WIDE].astype(F32)
            at = b * 256 + s * TOK
            xs_ref[at : at + TOK, :] = (x * grow[s * TOK : (s + 1) * TOK]).astype(BF16)
    row8 = iota((AUX, WIDE), 0)
    for d in range(2):
        tail = jnp.broadcast_to(jnp.where(key == last[d].astype(jnp.int32) + 4 * d, total, 0.0), (AUX, TOK))
        through = jnp.exp(-rate * dot(three(tail, lane), expand, ((1,), (0,))))
        e = dot(bt_ref[d], xs_ref[...], ((1,), (0,))) * through[0:1]
        e_ref[d, 0:WIDE, :] = e.astype(BF16)
        e_ref[d, WIDE : WIDE + AUX, :] = jnp.broadcast_to(last[d], (AUX, WIDE)).astype(BF16)
        own_ref[d] = jnp.where(row8 == 0, jnp.where(first[d] == last[d], through, 0.0), first[d])
    for copy in copies:
        copy.wait()


def decay_kernel(rate_ref, v_ref, f_ref):
    rate = rate_lanes(rate_ref)
    expand = ones_where(iota((TOK, WIDE), 0) % 4 == iota((TOK, WIDE), 1) // 64, BF16)
    for b in range(4):
        sl = slice(b * 256, (b + 1) * 256)
        f_ref[sl, :] = jnp.exp(-rate * dot(v_ref[sl, :], expand, ((1,), (0,)))).astype(BF16)


def inside_kernel(weight_ref, r_ref, got_ref, f_ref, xs_ref, base_ref, cm_ref, b_ref, c_ref):
    weight = rate_lanes(weight_ref)
    key_rows, key_cols, first = keys_of(r_ref)
    for q in range(PEERS):
        src = (q % 2) * 4 + q // 2
        sl = slice(q * TOK, (q + 1) * TOK)
        b_ref[sl, :] = r_ref[src, TOK:AT, :]
        c = got_ref[src]
        c_ref[sl, :] = c
        for d in range(2):
            fm = ones_where(key_cols[q] == first[d] + 4.0 * d, BF16)
            for half in range(2):
                at = d * WIDE + half * TOK
                cm_ref[sl, at : at + TOK] = c[:, half * TOK : (half + 1) * TOK] * fm
    causal = iota((256, 256), 0) >= iota((256, 256), 1)
    for i in range(4):
        si = slice(i * 256, (i + 1) * 256)
        acc = jnp.zeros((256, WIDE), F32)
        keys = jnp.concatenate([jnp.concatenate([key_cols[2 * i + n]] * 2, axis=1) for n in range(2)], axis=0)
        for j in range(i + 1):
            sj = slice(j * 256, (j + 1) * 256)
            s = dot(c_ref[si, :], b_ref[sj, :], ((1,), (1,)))
            same = keys == jnp.concatenate(key_rows[2 * j : 2 * j + 2], axis=1)
            w = jnp.where(same & causal if i == j else same, s, 0.0).astype(BF16)
            acc = acc + dot(w, xs_ref[sj, :], ((1,), (0,)))
        acc = acc * f_ref[si, :].astype(F32)
        for s in range(2):
            x = r_ref[s * 4 + i, :TOK, 0:WIDE].astype(F32)
            at = i * 256 + s * TOK
            base_ref[at : at + TOK, :] = acc[s * TOK : (s + 1) * TOK] + weight * x


def pass_kernel(e_ref, own_ref, out_ref):
    for d in range(2):
        joined = e_ref[d, WIDE : WIDE + 1, :].astype(F32) == own_ref[d, 1:2, :]
        through = jnp.where(joined, own_ref[d, 0:1, :], 0.0)
        out_ref[d] = (through * e_ref[d, 0:WIDE, :].astype(F32)).astype(BF16)


def carry_kernel(base_ref, f_ref, cm_ref, e1_ref, e2_ref, own_ref, y_ref, h_ref):
    for d in range(2):
        joined = e1_ref[d, WIDE : WIDE + 1, :].astype(F32) == own_ref[d, 1:2, :]
        h = e1_ref[d, 0:WIDE, :].astype(F32) + e2_ref[d].astype(F32)
        h_ref[d * WIDE : (d + 1) * WIDE, :] = jnp.where(joined, h, 0.0).astype(BF16)
    for q in range(PEERS):
        sl = slice(q * TOK, (q + 1) * TOK)
        y = base_ref[sl, :] + f_ref[sl, :].astype(F32) * dot(cm_ref[sl, :], h_ref[...], ((1,), (0,)))
        y_ref[(q % 2) * 4 + q // 2] = y.astype(BF16)


def square_kernel(y_ref, s_ref):
    acc = jnp.zeros((TOK, WIDE), F32)
    for o in range(PEERS):
        v = y_ref[o].astype(F32)
        acc = acc + v * v
    s_ref[...] = dot(jnp.ones((AUX, WIDE), F32), acc, ((1,), (1,)), HIGH)


def add_kernel(a_ref, b_ref, out_ref):
    out_ref[...] = a_ref[...] + b_ref[...]


def scale_kernel(y_ref, s0_ref, s1_ref, gain_ref, out_ref, *, features):
    total = s0_ref[...] + s1_ref[...]
    pick = ones_where(iota((AUX, TOK), 0) == 0)
    col = dot(total, pick, ((0,), (0,)), HIGH)
    scale = lax.rsqrt(col / features + EPSILON)
    scale = jnp.concatenate([scale, scale], axis=1)
    for o in range(PEERS):
        sl = slice(o * WIDE, (o + 1) * WIDE)
        out_ref[:, sl] = (y_ref[o].astype(F32) * scale * gain_ref[:, sl]).astype(BF16)


VM = pl.BlockSpec(memory_space=pltpu.VMEM)
SM = pl.BlockSpec(memory_space=pltpu.SMEM)
HB = pl.BlockSpec(memory_space=pl.ANY)


def kept(x):
    return pltpu.with_memory_space_constraint(x, pltpu.VMEM)


def far(x):
    return pltpu.with_memory_space_constraint(x, pltpu.HBM)


def call(kernel, specs, outs, *args, scratch=(), out_specs=None):
    return pl.pallas_call(
        kernel,
        in_specs=specs,
        out_specs=out_specs or [VM] * len(outs),
        out_shape=outs,
        scratch_shapes=list(scratch),
        compiler_params=pltpu.CompilerParams(vmem_limit_bytes=14 << 20),
    )(*args)


def whole(tokens, bc_proj, step_sizes, decay_rates, direct_weight, norm_gain, routes, segments):
    V = pltpu.VMEM
    pairs = bc_proj.reshape(TOK, 2, 4, TOK).transpose(0, 2, 1, 3).reshape(8 * TOK, TOK)
    send, send_c = call(
        pack_kernel,
        [HB] * 5,
        [V((PEERS, AT + AUX, WIDE), BF16), pltpu.HBM((PEERS, TOK, WIDE), BF16)],
        far(tokens[0]), far(pairs), far(step_sizes[0]), far(routes.reshape(1, 16)), far(segments),
        scratch=[
            V((8 * TOK, TOK), BF16),
            V((16, 256), BF16),
            V((1, 16), jnp.int32),
            V((1, 256), jnp.int32),
            V((8 * TOK, TOK), F32),
            V((2, TOK, WIDE), BF16),
            pltpu.SemaphoreType.DMA((4 + 2 * PEERS,)),
        ],
        out_specs=[VM, HB],
    )
    got = kept(lax.all_to_all(send, ("dp", "y"), split_axis=0, concat_axis=0, tiled=True))
    e, v, xs, own = call(
        state_kernel,
        [SM, VM],
        [V((2, WIDE + AUX, WIDE), BF16), pltpu.HBM((SPAN, TOK), BF16), V((SPAN, WIDE), BF16), V((2, AUX, WIDE), F32)],
        decay_rates, got,
        scratch=[V((2, WIDE, SPAN), BF16), V((SPAN, TOK), BF16), pltpu.SemaphoreType.DMA((4,))],
        out_specs=[VM, HB, VM, VM],
    )
    v, xs, own = far(v), kept(xs), kept(own)
    e, send_c = lax.optimization_barrier((e, send_c))
    e1 = kept(lax.ppermute(e, "z", [(i, i + 1) for i in range(3)]))
    got_c = kept(lax.all_to_all(send_c, ("dp", "y"), split_axis=0, concat_axis=0, tiled=True))
    (older,) = call(pass_kernel, [VM, VM], [V((2, WIDE, WIDE), BF16)], e1, own)
    e2 = kept(lax.ppermute(older, "z", [(i, i + 1) for i in range(1, 3)]))
    (f,) = call(decay_kernel, [SM, VM], [V((SPAN, WIDE), BF16)], decay_rates, v)
    f = kept(f)
    base, cm = call(
        inside_kernel,
        [SM] + [VM] * 4,
        [V((SPAN, WIDE), F32), V((SPAN, 2 * WIDE), BF16)],
        direct_weight, got, got_c, f, xs,
        scratch=[V((SPAN, WIDE), BF16), V((SPAN, WIDE), BF16)],
    )
    (out,) = call(
        carry_kernel,
        [VM] * 6,
        [V((PEERS, TOK, WIDE), BF16)],
        kept(base), f, kept(cm), e1, e2, own,
        scratch=[V((2 * WIDE, WIDE), BF16)],
    )
    back = kept(lax.all_to_all(out, ("dp", "y"), split_axis=0, concat_axis=0, tiled=True))
    (s0,) = call(square_kernel, [VM], [V((AUX, TOK), F32)], back)
    t0 = lax.ppermute(s0, "tensor", [(i, i ^ 1) for i in range(4)])
    (s0,) = call(add_kernel, [VM] * 2, [V((AUX, TOK), F32)], kept(s0), kept(t0))
    others = [kept(lax.ppermute(s0, "tensor", [(i, i ^ 2) for i in range(4)]))]

    def scale(*refs):
        scale_kernel(*refs, features=128 * 64)

    out_shape = [jax.ShapeDtypeStruct((TOK, PEERS * WIDE), BF16)]
    (mixed,) = call(scale, [VM] * 4, out_shape, back, kept(s0), *others, norm_gain[None])
    return mixed[None]


def solution(mesh):
    fine = Mesh(mesh.devices.reshape(2, 4, 4, 4), ("dp", "z", "y", "tensor"))
    rows = ("z", "y")
    return jax.shard_map(
        whole,
        mesh=fine,
        in_specs=(
            P("dp", rows, "tensor"),
            P("dp", rows, None, "tensor"),
            P("dp", rows, "tensor"),
            P("tensor"),
            P("tensor"),
            P("tensor"),
            P("dp", rows, None),
            P("dp", rows),
        ),
        out_specs=P("dp", rows, "tensor"),
        check_vma=False,
    )
```
